128 devices in a mesh: harm: 8 (over x_hi, y), gx: 4 (over z), gz: 4 (over x_lo, core).
Axes of the slice: x: 4 (x_hi: 2, x_lo: 2; x = x_hi * 2 + x_lo), y: 4, z: 4, core: 2. Of those that a mesh axis runs over, the one named last changes fastest.
Arguments:
- perturbation: bfloat16 [32, 2, 4, 128, 24, 128], P('harm', None, None, 'gx', 'gz'), may hold values from -6 to 6
- base_mean: bfloat16 [3, 128, 24, 128], P(None, 'gx', 'gz'), may hold values from -6 to 6
- base_modes: bfloat16 [2, 2, 3, 128, 24, 128], P(None, None, None, 'gx', 'gz'), may hold values from -3 to 3
- solid_mask: int32 [128, 24, 128], P('gx', 'gz'), may hold values from 0 to 1, as said below
Outputs:
- residual_harmonics: float32 [32, 2, 4, 128, 24, 128], P('harm', None, None, 'gx', 'gz')
The draws below stay inside these ranges and needn't reach their ends.
Inputs may be any that keep to these rules, and one draw needn't show every extreme that they name: `solid_mask`: 1 on the cells of one circular cylinder of radius 2 or more cells in the x-y plane, the same at every spanwise position, 0 elsewhere.
All inputs are finite; a program needn't handle non-finite values.
Results may differ from the reference program's by a relative error of at most 0.0003.
Values may be sent and summed in bfloat16 or wider, within the bound.
A program may use at most 128 MiB of HBM per device.

```python
import jax
import jax.numpy as jnp
from jax import lax

MODES = 2
NY = 128
HARMS = 32
NX = 128
NZ = 24


def draw_solid_mask(key, part):
    key_x, key_y, key_r = jax.random.split(jax.random.fold_in(key, 17), 3)
    centre_x = jax.random.randint(key_x, (), 0, NX)
    centre_y = jax.random.randint(key_y, (), NY // 4, 3 * NY // 4)
    radius = jax.random.randint(key_r, (), 2, max(3, NY // 8) + 1)
    spots_x = jnp.arange(NX, dtype=jnp.int32)[:, None]
    spots_y = jnp.arange(NY, dtype=jnp.int32)[None, :]
    inside = (spots_x - centre_x) ** 2 + (spots_y - centre_y) ** 2 <= radius * radius
    plane = jnp.where(inside, 1, 0).astype(jnp.int32)
    return jnp.broadcast_to(plane[:, None, :], (NX, NZ, NY)).astype(jnp.int32)


def block_levels(rng, shape, pieces, smallest, largest):
    level, own = 1.0, jax.random.fold_in(rng, 6)
    for position, shards_of in pieces:
        heights = jnp.exp(jax.random.uniform(jax.random.fold_in(own, position), (shards_of,), jnp.float32, smallest / len(pieces), largest / len(pieces)))
        level = level * jnp.repeat(heights, shape[position] // shards_of).reshape([-1 if axis == position else 1 for axis in range(len(shape))])
    return level


def centred(own_key, shape, deviation, reach, pieces=(), kind=jnp.bfloat16):
    drawn = deviation * jax.random.normal(own_key, shape, jnp.float32)
    if pieces:
        drawn = drawn * block_levels(own_key, shape, pieces, -0.22, 0.18)
    return jnp.clip(drawn, -reach, reach).astype(kind)


def setup_inputs(seed: int = 0) -> dict:
    keys = jax.random.split(jax.random.key(seed), 5)
    return {
        "perturbation": centred(keys[0], (HARMS, 2, 4, NX, NZ, NY), 1.0, 6.0, ((0, 8), (3, 4), (4, 4))),
        "base_mean": centred(keys[1], (3, NX, NZ, NY), 1.0, 6.0, ((1, 4), (2, 4))),
        "base_modes": centred(keys[2], (MODES, 2, 3, NX, NZ, NY), 0.5, 3.0, ((3, 4), (4, 4))),
        "solid_mask": draw_solid_mask(jax.random.fold_in(keys[4], 71), 0),
    }


FREQUENCY_STEP = 0.2
VISCOSITY = 0.05
PENALTY = 4.0


def wall_shift(values, offset):
    dims_count = values.ndim
    length_y = values.shape[-1]
    widths = [(0, 0)] * (dims_count - 1) + [(2, 2)]
    return lax.slice_in_dim(jnp.pad(values, widths), 2 + offset, 2 + offset + length_y, axis=dims_count - 1)


def moved(values, direction, offset):
    if direction == 0:
        return jnp.roll(values, -offset, axis=values.ndim - 3)
    if direction == 2:
        return jnp.roll(values, -offset, axis=values.ndim - 2)
    return wall_shift(values, offset)


def first_deriv(values, direction):
    near = moved(values, direction, 1) - moved(values, direction, -1)
    far = moved(values, direction, 2) - moved(values, direction, -2)
    return (8.0 * near - far) / 12.0


def second_deriv(values, direction):
    near = moved(values, direction, 1) + moved(values, direction, -1)
    far = moved(values, direction, 2) + moved(values, direction, -2)
    return (16.0 * near - far - 30.0 * values) / 12.0


def base_pair(mean_part, mode_part, mode_shift):
    if mode_shift == 0:
        return mean_part, jnp.zeros_like(mean_part)
    if mode_shift > 0:
        return mode_part[mode_shift - 1, 0], mode_part[mode_shift - 1, 1]
    return mode_part[-mode_shift - 1, 0], -mode_part[-mode_shift - 1, 1]


def reference(perturbation, base_mean, base_modes, solid_mask):
    values = perturbation.astype(jnp.float32)
    velocity = values[:, :, :3]
    pressure = values[:, :, 3]
    count_h = values.shape[0]
    blank = jnp.zeros((MODES,) + velocity.shape[1:], jnp.float32)
    extended = jnp.concatenate([blank, velocity, blank], 0)
    mean_flow = base_mean.astype(jnp.float32)
    mode_flow = base_modes.astype(jnp.float32)
    solid_field = solid_mask.astype(jnp.float32)
    harmonic = jnp.arange(count_h, dtype=jnp.int32) - count_h // 2
    frequency = (FREQUENCY_STEP * harmonic.astype(jnp.float32))[:, None, None, None, None]
    accum_real = -frequency * velocity[:, 1] + PENALTY * solid_field * velocity[:, 0]
    accum_imag = frequency * velocity[:, 0] + PENALTY * solid_field * velocity[:, 1]
    diverge_real = jnp.zeros(pressure[:, 0].shape, jnp.float32)
    diverge_imag = jnp.zeros(pressure[:, 0].shape, jnp.float32)
    for direction in range(3):
        gradient = first_deriv(extended, direction)
        mean_grad = first_deriv(mean_flow, direction)
        mode_grad = first_deriv(mode_flow, direction)
        press_grad = first_deriv(pressure, direction)
        laplace_term = second_deriv(velocity, direction)
        selector = (jnp.arange(3, dtype=jnp.int32) == direction).astype(jnp.float32)[:, None, None, None]
        accum_real = accum_real + press_grad[:, 0][:, None] * selector - VISCOSITY * laplace_term[:, 0]
        accum_imag = accum_imag + press_grad[:, 1][:, None] * selector - VISCOSITY * laplace_term[:, 1]
        diverge_real = diverge_real + gradient[MODES:MODES + count_h, 0, direction]
        diverge_imag = diverge_imag + gradient[MODES:MODES + count_h, 1, direction]
        for mode_shift in range(-MODES, MODES + 1):
            flow_real, flow_imag = base_pair(mean_flow, mode_flow, mode_shift)
            slope_real, slope_imag = base_pair(mean_grad, mode_grad, mode_shift)
            grad_src = gradient[MODES - mode_shift:MODES - mode_shift + count_h]
            value_src = extended[MODES - mode_shift:MODES - mode_shift + count_h]
            carry_real = flow_real[direction]
            carry_imag = flow_imag[direction]
            along_real = value_src[:, 0, direction][:, None]
            along_imag = value_src[:, 1, direction][:, None]
            accum_real = accum_real + carry_real * grad_src[:, 0] - carry_imag * grad_src[:, 1] + along_real * slope_real - along_imag * slope_imag
            accum_imag = accum_imag + carry_real * grad_src[:, 1] + carry_imag * grad_src[:, 0] + along_real * slope_imag + along_imag * slope_real
    momentum = jnp.stack([accum_real, accum_imag], 1)
    continuity = jnp.stack([diverge_real, diverge_imag], 1)[:, :, None]
    return jnp.concatenate([momentum, continuity], 2)
```

```python
import jax
import jax.numpy as jnp
from jax import lax
from jax.experimental import pallas as pl
from jax.experimental.pallas import tpu as pltpu
from jax.sharding import PartitionSpec as P

FREQUENCY_STEP = 0.2
VISCOSITY = 0.05
PENALTY = 4.0
EDGE = 8
ROWS = 48


def with_halo(shard, sides, width, wrap):
    for axis, dim in sides:
        size, length = (lax.axis_size(axis), shard.shape[dim])
        up = [(i, (i + 1) % size) for i in range(size if wrap else size - 1)]
        down = [(j, i) for i, j in up]
        last = lax.slice_in_dim(shard, length - width, length, axis=dim)
        first = lax.slice_in_dim(shard, 0, width, axis=dim)
        before = lax.ppermute(last, axis, up)
        after = lax.ppermute(first, axis, down)
        shard = jnp.concatenate([before, shard, after], axis=dim)
    return shard


def vel(l, part, c):
    return (l * 2 + part) * 3 + c


def pres(l, part):
    return 48 + l * 2 + part


def base(m, part, c):
    return 56 + c if m == 0 else 59 + ((m - 1) * 2 + part) * 3 + c


def block(slabs, mask_ref, out_ref, masks, freqs, z, xb):
    row = xb * 8 + EDGE

    def load(field, dz=0, dx=0):
        return slabs[field, z + 2 + dz, pl.ds(row + dx, 8), :]

    def lane(value, offset):
        return jnp.where(masks[offset], pltpu.roll(value, (-offset) % 128, 1), 0.0)

    def sides(field, d):
        if d == 0:
            return tuple(load(field, 0, o) for o in (1, -1, 2, -2))
        if d == 2:
            return tuple(load(field, o, 0) for o in (1, -1, 2, -2))
        value = load(field)
        return tuple(lane(value, o) for o in (1, -1, 2, -2))

    def slope(s):
        return 8.0 * (s[0] - s[1]) - (s[2] - s[3])

    solid = PENALTY * mask_ref[z, pl.ds(xb * 8, 8), :].astype(jnp.float32)
    flow = {
        (m, part, d): load(base(m, part, d)) * (1.0 / 12.0)
        for m in range(3)
        for part in range(1 if m == 0 else 2)
        for d in range(3)
    }
    diverge = {}
    for c in range(3):
        bend = {
            (m, part, d): slope(sides(base(m, part, c), d)) * (1.0 / 12.0)
            for m in range(3)
            for part in range(1 if m == 0 else 2)
            for d in range(3)
        }
        total = {}
        for l in range(8):
            own = 2 <= l < 6
            grad = {}
            for part in range(2):
                around = [sides(vel(l, part, c), d) for d in range(3)]
                for d in range(3):
                    grad[part, d] = slope(around[d])
                if own:
                    value = load(vel(l, part, c))
                    near = sum(s[0] + s[1] for s in around)
                    far = sum(s[2] + s[3] for s in around)
                    other = load(vel(l, 1 - part, c))
                    turn = freqs[l - 2] * other
                    start = (
                        solid * value
                        - (VISCOSITY * 16.0 / 12.0) * near
                        + (VISCOSITY / 12.0) * far
                        + (VISCOSITY * 90.0 / 12.0) * value
                    )
                    start = start - turn if part == 0 else start + turn
                    k = l - 2
                    start = start + slope(sides(pres(k, part), c)) * (1.0 / 12.0)
                    total[k, part] = start + total[k, part] if (k, part) in total else start
                    key = (k, part)
                    diverge[key] = grad[part, c] + diverge[key] if key in diverge else grad[part, c]
            speed = {(part, d): load(vel(l, part, d)) for part in range(2) for d in range(3)}
            for k in range(4):
                m = k - (l - 2)
                if abs(m) > 2:
                    continue
                a = abs(m)
                pieces_r, pieces_i = [], []
                for d in range(3):
                    gr, gi = grad[0, d], grad[1, d]
                    ur, ui = speed[0, d], speed[1, d]
                    fr, br = flow[a, 0, d], bend[a, 0, d]
                    pieces_r += [fr * gr, ur * br]
                    pieces_i += [fr * gi, ui * br]
                    if a:
                        fi, bi = flow[a, 1, d], bend[a, 1, d]
                        sign = 1 if m > 0 else -1
                        pieces_r += [(-sign, fi * gi), (-sign, ui * bi)]
                        pieces_i += [(sign, fi * gr), (sign, ur * bi)]
                for part, pieces in ((0, pieces_r), (1, pieces_i)):
                    value = total.get((k, part))
                    for piece in pieces:
                        sign, term = piece if isinstance(piece, tuple) else (1, piece)
                        if value is None:
                            value = term if sign > 0 else -term
                        else:
                            value = value + term if sign > 0 else value - term
                    total[k, part] = value
        for k in range(4):
            for part in range(2):
                out_ref[k, part, c, z, pl.ds(xb * 8, 8), :] = total[k, part]
    for k in range(4):
        for part in range(2):
            out_ref[k, part, 3, z, pl.ds(xb * 8, 8), :] = diverge[k, part] * (1.0 / 12.0)


def kernel(vel_ref, pres_ref, base_ref, mask_ref, out_ref, slabs):
    harm = lax.axis_index("harm")
    freqs = [FREQUENCY_STEP * (harm * 4 + k - 16).astype(jnp.float32) for k in range(4)]

    def stage(ref, count, first):
        def body(i, carry):
            slabs[first + i] = ref[i].astype(jnp.float32)
            return carry

        lax.fori_loop(0, count, body, 0)

    stage(vel_ref, 48, 0)
    stage(pres_ref, 8, 48)
    stage(base_ref, 15, 56)
    lanes = lax.broadcasted_iota(jnp.int32, (8, 128), 1)
    masks = {1: lanes < 127, 2: lanes < 126, -1: lanes >= 1, -2: lanes >= 2}

    def layer(z, carry):
        def chunk(xb, inner):
            block(slabs, mask_ref, out_ref, masks, freqs, z, xb)
            return inner

        return lax.fori_loop(0, 4, chunk, carry)

    lax.fori_loop(0, 6, layer, 0)


def shards(perturbation, base_mean, base_modes, solid_mask):
    turned = jnp.transpose(perturbation, (0, 1, 2, 4, 3, 5))
    mean = jnp.transpose(base_mean, (0, 2, 1, 3))
    modes = jnp.transpose(base_modes, (0, 1, 2, 4, 3, 5))
    mask = jnp.transpose(solid_mask, (1, 0, 2))
    per, _, _, cz, cx, cy = turned.shape
    base_all = jnp.concatenate([mean, modes.reshape(12, cz, cx, cy)], 0)
    velocity = with_halo(turned[:, :, :3], (("harm", 0),), 2, False)
    pressure = turned[:, :, 3].reshape(per * 2, cz, cx, cy)
    velocity = velocity.reshape(48, cz, cx, cy)

    def pad(values):
        values = with_halo(values, (("gx", 2), ("gz", 1)), 2, True)
        return jnp.pad(values, ((0, 0), (0, 0), (6, 6), (0, 0)))

    vmem = pl.BlockSpec(memory_space=pltpu.VMEM)
    out = pl.pallas_call(
        kernel,
        out_shape=jax.ShapeDtypeStruct((per, 2, 4, cz, cx, cy), jnp.float32),
        in_specs=[vmem] * 4,
        out_specs=vmem,
        scratch_shapes=[pltpu.VMEM((71, 10, ROWS, 128), jnp.float32)],
        compiler_params=pltpu.CompilerParams(vmem_limit_bytes=60 * 1024 * 1024),
    )(pad(velocity), pad(pressure), pad(base_all), mask)
    return jnp.transpose(out, (0, 1, 2, 4, 3, 5))


def solution(mesh):
    return jax.shard_map(
        shards,
        mesh=mesh,
        in_specs=(
            P("harm", None, None, "gx", "gz", None),
            P(None, "gx", "gz", None),
            P(None, None, None, "gx", "gz", None),
            P("gx", "gz", None),
        ),
        out_specs=P("harm", None, None, "gx", "gz", None),
        check_vma=False,
    )
```

```python
import jax
import jax.numpy as jnp
from jax import lax
from jax.experimental import pallas as pl
from jax.experimental.pallas import tpu as pltpu
from jax.sharding import PartitionSpec as P

FREQUENCY_STEP = 0.2
VISCOSITY = 0.05
PENALTY = 4.0
TWELFTH = 1.0 / 12.0
MESH = pl.DeviceIdType.MESH

LAYERS, ROWS, LANES = 10, 48, 128
OWN_Z = pl.ds(2, 6)
OWN_X = pl.ds(8, 32)
RIM_Z = {1: pl.ds(0, 2), -1: pl.ds(8, 2)}
RIM_X = {1: pl.ds(6, 2), -1: pl.ds(40, 2)}
BARE_Z = {1: pl.ds(4, 2), -1: pl.ds(0, 2)}
BARE_X = {1: pl.ds(30, 2), -1: pl.ds(0, 2)}
SLAB_Z = {1: pl.ds(6, 2), -1: pl.ds(2, 2)}
SLAB_X = {1: pl.ds(38, 2), -1: pl.ds(8, 2)}

OWN0, LOW0, HIGH0, BASE0, FIELDS = 0, 32, 44, 56, 71


def vel(l, part, c):
    if l < 0:
        return LOW0 + ((l + 2) * 2 + part) * 3 + c
    if l > 3:
        return HIGH0 + ((l - 4) * 2 + part) * 3 + c
    return OWN0 + (l * 2 + part) * 4 + c


def base(m, part, c):
    return BASE0 + (c if m == 0 else 3 + ((m - 1) * 2 + part) * 3 + c)


MODES = [(0, 0), (1, 0), (1, 1), (2, 0), (2, 1)]
OWN = (0, 1, 2, 3)
OTHERS = (-2, -1, 4, 5)


def block(slabs, mask, out, masks, freqs, z, xb, jobs, first):
    row = xb * 8 + 8
    here = pl.ds(xb * 8, 8)

    def load(field, dz=0, dx=0):
        return slabs[field, z + 2 + dz, pl.ds(row + dx, 8), :]

    def lane(value, offset):
        return jnp.where(masks[offset], pltpu.roll(value, (-offset) % LANES, 1), 0.0)

    def sides(field, d):
        if d == 0:
            return tuple(load(field, 0, o) for o in (1, -1, 2, -2))
        if d == 2:
            return tuple(load(field, o, 0) for o in (1, -1, 2, -2))
        value = load(field)
        return tuple(lane(value, o) for o in (1, -1, 2, -2))

    def slope(s):
        return 8.0 * (s[0] - s[1]) - (s[2] - s[3])

    used = sorted({d for _, dirs in jobs for d in dirs})
    flow = {(m, part, d): load(base(m, part, d)) * TWELFTH for m, part in MODES for d in used}
    solid = PENALTY * mask[z, here, :].astype(jnp.float32) if first else None
    diverge = {}
    for c in range(3):
        bend = {(m, part, d): slope(sides(base(m, part, c), d)) * TWELFTH for m, part in MODES for d in used}
        total = {}
        if not first:
            total = {(k, part): out[k, part, c, z, here, :] for k in OWN for part in range(2)}

        def add(key, term):
            total[key] = total[key] + term if key in total else term

        def sub(key, term):
            total[key] = total[key] - term if key in total else -term

        for ls, dirs in jobs:
            for l in ls:
                grad = {}
                for part in range(2):
                    around = {d: sides(vel(l, part, c), d) for d in dirs}
                    for d in dirs:
                        grad[part, d] = slope(around[d])
                    if l in OWN:
                        key = (l, part)
                        near = sum(around[d][0] + around[d][1] for d in dirs)
                        far = sum(around[d][2] + around[d][3] for d in dirs)
                        sub(key, (VISCOSITY * 16.0 * TWELFTH) * near)
                        add(key, (VISCOSITY * TWELFTH) * far)
                        if 0 in dirs:
                            value = load(vel(l, part, c))
                            add(key, (solid + VISCOSITY * 90.0 * TWELFTH) * value)
                            turn = freqs[l] * load(vel(l, 1 - part, c))
                            (sub if part == 0 else add)(key, turn)
                        if c in dirs:
                            add(key, slope(sides(OWN0 + (l * 2 + part) * 4 + 3, c)) * TWELFTH)
                            diverge[key] = diverge[key] + grad[part, c] if key in diverge else grad[part, c]
                speed = {(part, d): load(vel(l, part, d)) for part in range(2) for d in dirs}
                for k in OWN:
                    m = k - l
                    if abs(m) > 2:
                        continue
                    a = abs(m)
                    for d in dirs:
                        gr, gi = grad[0, d], grad[1, d]
                        ur, ui = speed[0, d], speed[1, d]
                        fr, br = flow[a, 0, d], bend[a, 0, d]
                        add((k, 0), fr * gr + ur * br)
                        add((k, 1), fr * gi + ui * br)
                        if a:
                            fi, bi = flow[a, 1, d], bend[a, 1, d]
                            real, imag = fi * gi + ui * bi, fi * gr + ur * bi
                            (sub if m > 0 else add)((k, 0), real)
                            (add if m > 0 else sub)((k, 1), imag)
        for key, value in total.items():
            out[key[0], key[1], c, z, here, :] = value
    for (k, part), value in diverge.items():
        value = value * TWELFTH
        out[k, part, 3, z, here, :] = value if first else out[k, part, 3, z, here, :] + value


def kernel(pert, mean, modes, solid_hbm, out_hbm, own, low, high, flow, slabs, out, solid, local_sem, send_sem, recv_sem, out_sem):
    h, gx, gz = lax.axis_index("harm"), lax.axis_index("gx"), lax.axis_index("gz")
    side_x = {1: lax.rem(gx + 1, 4), -1: lax.rem(gx + 3, 4)}
    side_z = {1: lax.rem(gz + 1, 4), -1: lax.rem(gz + 3, 4)}
    odd = lax.rem(gz, 2)
    twin = {1: lax.rem(h + 4 * odd, 8), -1: lax.rem(h + 4 * (1 - odd), 8)}
    has_low, has_high = h > 0, h < 7

    barrier = pltpu.get_barrier_semaphore()

    def greet(device):
        pl.semaphore_signal(barrier, inc=1, device_id=device, device_id_type=MESH)

    for s in (1, -1):
        greet((h, side_x[s], gz))
        greet((h, gx, side_z[s]))
    greet((lax.rem(h + 4, 8), gx, 3 - gz))

    @pl.when(has_low)
    def _():
        greet((h - 1, gx, gz))

    @pl.when(has_high)
    def _():
        greet((h + 1, gx, gz))

    def local(i, src, dst):
        return pltpu.make_async_copy(src, dst, local_sem.at[i])

    loads = [
        local(0, pert, own.at[:, :, :, OWN_Z, OWN_X]),
        local(1, mean, flow.at[pl.ds(0, 3), OWN_Z, OWN_X]),
        local(2, modes.at[0, 0], flow.at[pl.ds(3, 3), OWN_Z, OWN_X]),
        local(3, modes.at[0, 1], flow.at[pl.ds(6, 3), OWN_Z, OWN_X]),
        local(4, modes.at[1, 0], flow.at[pl.ds(9, 3), OWN_Z, OWN_X]),
        local(5, modes.at[1, 1], flow.at[pl.ds(12, 3), OWN_Z, OWN_X]),
        local(6, solid_hbm, solid),
    ]
    for copy in loads:
        copy.start()

    pl.semaphore_wait(barrier, 5 + jnp.where(has_low, 1, 0) + jnp.where(has_high, 1, 0))

    counter = iter(range(64))

    def remote(src, dst, device):
        i = next(counter)
        return pltpu.make_async_remote_copy(
            src_ref=src, dst_ref=dst, send_sem=send_sem.at[i], recv_sem=recv_sem.at[i], device_id=device, device_id_type=MESH
        )

    three = pl.ds(0, 3)
    tile = (slice(None), slice(None), slice(None), OWN_Z, OWN_X)
    up = remote(pert.at[pl.ds(2, 2), :, three], low.at[tile], (jnp.minimum(h + 1, 7), gx, gz))
    down = remote(pert.at[pl.ds(0, 2), :, three], high.at[tile], (jnp.maximum(h - 1, 0), gx, gz))
    rim_x, rim_z, base_x, base_z = [], [], [], []
    for s in (1, -1):
        rim_z.append(remote(pert.at[:, :, :, BARE_Z[s]], own.at[:, :, :, RIM_Z[s], OWN_X], (h, gx, side_z[s])))
        rim_x.append(remote(pert.at[:, :, :, :, BARE_X[s]], own.at[:, :, :, OWN_Z, RIM_X[s]], (h, side_x[s], gz)))
        pieces = [(mean, 0)] + [(modes.at[m, part], 3 + (m * 2 + part) * 3) for m in range(2) for part in range(2)]
        for ref, at in pieces:
            fields = pl.ds(at, 3)
            base_x.append(remote(ref.at[:, :, BARE_X[s]], flow.at[fields, OWN_Z, RIM_X[s]], (h, side_x[s], gz)))
            base_z.append(remote(ref.at[:, BARE_Z[s]], flow.at[fields, RIM_Z[s], OWN_X], (twin[s], gx, side_z[s])))
    pl.when(has_high)(up.start)
    pl.when(has_low)(down.start)
    for copy in rim_x + rim_z + base_x + base_z:
        copy.start()
    corner = {}
    for name, ref in (("low", low), ("high", high)):
        corner[name, "x"] = [
            remote(ref.at[:, :, :, OWN_Z, SLAB_X[s]], ref.at[:, :, :, OWN_Z, RIM_X[s]], (h, side_x[s], gz)) for s in (1, -1)
        ]
        corner[name, "z"] = [
            remote(ref.at[:, :, :, SLAB_Z[s], OWN_X], ref.at[:, :, :, RIM_Z[s], OWN_X], (h, gx, side_z[s])) for s in (1, -1)
        ]

    def stage(ref, shape, first, layers, rows):
        def body(i, carry):
            index, rest = [], i
            for size in reversed(shape):
                index.insert(0, lax.rem(rest, size))
                rest = lax.div(rest, size)
            for z in layers:
                slabs[first + i, z, rows, :] = ref[(*index, z, rows)].astype(jnp.float32)
            return carry

        count = 1
        for size in shape:
            count *= size
        lax.fori_loop(0, count, body, 0)

    middle, edge = range(2, 8), (0, 1, 8, 9)
    every = pl.ds(0, ROWS)
    for copy in loads:
        copy.wait()
    for copy in rim_x + base_x:
        copy.wait_recv()
    stage(own, (4, 2, 4), OWN0, middle, every)
    stage(flow, (15,), BASE0, middle, every)

    lanes = lax.broadcasted_iota(jnp.int32, (8, LANES), 1)
    masks = {1: lanes < LANES - 1, 2: lanes < LANES - 2, -1: lanes >= 1, -2: lanes >= 2}
    freqs = [FREQUENCY_STEP * (h * 4 + k - 16).astype(jnp.float32) for k in range(4)]

    def sweep(jobs, first, finish=None):
        def layer(z, carry):
            def chunk(xb, inner):
                block(slabs, solid, out, masks, freqs, z, xb, jobs, first)
                return inner

            lax.fori_loop(0, 4, chunk, 0)
            if finish is not None:
                finish(z)
            return carry

        lax.fori_loop(0, 6, layer, 0)

    sweep([(OWN, (0, 1))], True)

    def relay(present, ref, name, arrival, first):
        @pl.when(present)
        def _():
            arrival.wait_recv()
            for copy in corner[name, "z"] + corner[name, "x"]:
                copy.start()

    relay(has_low, low, "low", up, LOW0)
    relay(has_high, high, "high", down, HIGH0)
    for copy in rim_z + base_z:
        copy.wait_recv()
    stage(own, (4, 2, 4), OWN0, edge, OWN_X)
    stage(flow, (15,), BASE0, edge, OWN_X)
    sweep([(OWN, (2,))], False)

    def settle(present, ref, name, first):
        @pl.when(present)
        def _():
            for copy in corner[name, "z"] + corner[name, "x"]:
                copy.wait_recv()
            stage(ref, (2, 2, 3), first, middle, every)
            stage(ref, (2, 2, 3), first, edge, OWN_X)

        @pl.when(jnp.logical_not(present))
        def _():
            def clear(i, carry):
                slabs[first + i] = jnp.zeros((LAYERS, ROWS, LANES), jnp.float32)
                return carry

            lax.fori_loop(0, 12, clear, 0)

    settle(has_low, low, "low", LOW0)
    settle(has_high, high, "high", HIGH0)

    def write(z):
        return pltpu.make_async_copy(out.at[:, :, :, z], out_hbm.at[:, :, :, z], out_sem.at[z])

    sweep([(OTHERS, (0, 1, 2))], False, lambda z: write(z).start())

    def drain(z, carry):
        write(z).wait()
        return carry

    lax.fori_loop(0, 6, drain, 0)
    for copy in rim_x + rim_z + base_x + base_z:
        copy.wait_send()
    pl.when(has_high)(up.wait_send)
    pl.when(has_low)(down.wait_send)
    for present, name in ((has_low, "low"), (has_high, "high")):

        @pl.when(present)
        def _(name=name):
            for copy in corner[name, "z"] + corner[name, "x"]:
                copy.wait_send()


def shards(perturbation, base_mean, base_modes, solid_mask):
    turned = jnp.transpose(perturbation, (0, 1, 2, 4, 3, 5))
    mean = jnp.transpose(base_mean, (0, 2, 1, 3))
    modes = jnp.transpose(base_modes, (0, 1, 2, 4, 3, 5))
    mask = jnp.transpose(solid_mask, (1, 0, 2))
    anywhere = pl.BlockSpec(memory_space=pl.ANY)
    half = jnp.bfloat16
    out = pl.pallas_call(
        kernel,
        out_shape=jax.ShapeDtypeStruct(turned.shape, jnp.float32),
        in_specs=[anywhere] * 4,
        out_specs=anywhere,
        scratch_shapes=[
            pltpu.VMEM((4, 2, 4, LAYERS, ROWS, LANES), half),
            pltpu.VMEM((2, 2, 3, LAYERS, ROWS, LANES), half),
            pltpu.VMEM((2, 2, 3, LAYERS, ROWS, LANES), half),
            pltpu.VMEM((15, LAYERS, ROWS, LANES), half),
            pltpu.VMEM((FIELDS, LAYERS, ROWS, LANES), jnp.float32),
            pltpu.VMEM(turned.shape, jnp.float32),
            pltpu.VMEM(mask.shape, jnp.int32),
            pltpu.SemaphoreType.DMA((7,)),
            pltpu.SemaphoreType.DMA((34,)),
            pltpu.SemaphoreType.DMA((34,)),
            pltpu.SemaphoreType.DMA((6,)),
        ],
        compiler_params=pltpu.CompilerParams(collective_id=0, has_side_effects=True, vmem_limit_bytes=60 * 1024 * 1024),
    )(turned, mean, modes, mask)
    return jnp.transpose(out, (0, 1, 2, 4, 3, 5))


def solution(mesh):
    return jax.shard_map(
        shards,
        mesh=mesh,
        in_specs=(
            P("harm", None, None, "gx", "gz", None),
            P(None, "gx", "gz", None),
            P(None, None, None, "gx", "gz", None),
            P("gx", "gz", None),
        ),
        out_specs=P("harm", None, None, "gx", "gz", None),
        check_vma=False,
    )
```

```python
import jax
import jax.numpy as jnp
from jax import lax
from jax.experimental import pallas as pl
from jax.experimental.pallas import tpu as pltpu
from jax.sharding import PartitionSpec as P

FREQUENCY_STEP = 0.2
VISCOSITY = 0.05
PENALTY = 4.0
TWELFTH = 1.0 / 12.0
MESH = pl.DeviceIdType.MESH

LAYERS, ROWS, LANES = 10, 48, 128
OWN_Z = pl.ds(2, 6)
OWN_X = pl.ds(8, 32)
RIM_Z = {1: pl.ds(0, 2), -1: pl.ds(8, 2)}
RIM_X = {1: pl.ds(6, 2), -1: pl.ds(40, 2)}
BARE_Z = {1: pl.ds(4, 2), -1: pl.ds(0, 2)}
BARE_X = {1: pl.ds(30, 2), -1: pl.ds(0, 2)}
SLAB_Z = {1: pl.ds(6, 2), -1: pl.ds(2, 2)}
SLAB_X = {1: pl.ds(38, 2), -1: pl.ds(8, 2)}

OWN0, LOW0, HIGH0, BASE0, FIELDS = 0, 32, 44, 56, 71


def vel(l, part, c):
    if l < 0:
        return LOW0 + ((l + 2) * 2 + part) * 3 + c
    if l > 3:
        return HIGH0 + ((l - 4) * 2 + part) * 3 + c
    return OWN0 + (l * 2 + part) * 4 + c


def base(m, part, c):
    return BASE0 + (c if m == 0 else 3 + ((m - 1) * 2 + part) * 3 + c)


MODES = [(0, 0), (1, 0), (1, 1), (2, 0), (2, 1)]
OWN = (0, 1, 2, 3)
OTHERS = (-2, -1, 4, 5)


def block(slabs, mask, out, masks, freqs, z, xb, jobs, first):
    row = xb * 8 + 8
    here = pl.ds(xb * 8, 8)

    def load(field, dz=0, dx=0):
        return slabs[field, z + 2 + dz, pl.ds(row + dx, 8), :]

    def lane(value, offset):
        return jnp.where(masks[offset], pltpu.roll(value, (-offset) % LANES, 1), 0.0)

    def sides(field, d):
        if d == 0:
            return tuple(load(field, 0, o) for o in (1, -1, 2, -2))
        if d == 2:
            return tuple(load(field, o, 0) for o in (1, -1, 2, -2))
        value = load(field)
        return tuple(lane(value, o) for o in (1, -1, 2, -2))

    def slope(s):
        return 8.0 * (s[0] - s[1]) - (s[2] - s[3])

    used = sorted({d for _, dirs in jobs for d in dirs})
    flow = {(m, part, d): load(base(m, part, d)) for m, part in MODES for d in used}
    solid = PENALTY * mask[z, here, :].astype(jnp.float32) if first else None
    diverge = {}
    for c in range(3):
        bend = {(m, part, d): slope(sides(base(m, part, c), d)) for m, part in MODES for d in used}
        total = {}
        if not first:
            total = {(k, part): out[k, part, c, z, here, :] for k in OWN for part in range(2)}

        def add(key, term):
            total[key] = total[key] + term if key in total else term

        def sub(key, term):
            total[key] = total[key] - term if key in total else -term

        for ls, dirs in jobs:
            for l in ls:
                grad = {}
                for part in range(2):
                    around = {d: sides(vel(l, part, c), d) for d in dirs}
                    for d in dirs:
                        grad[part, d] = slope(around[d])
                    if l in OWN:
                        key = (l, part)
                        near = sum(around[d][0] + around[d][1] for d in dirs)
                        far = sum(around[d][2] + around[d][3] for d in dirs)
                        sub(key, (VISCOSITY * 16.0 * TWELFTH) * near)
                        add(key, (VISCOSITY * TWELFTH) * far)
                        if 0 in dirs:
                            value = load(vel(l, part, c))
                            add(key, (solid + VISCOSITY * 90.0 * TWELFTH) * value)
                            turn = freqs[l] * load(vel(l, 1 - part, c))
                            (sub if part == 0 else add)(key, turn)
                        if c in dirs:
                            add(key, slope(sides(OWN0 + (l * 2 + part) * 4 + 3, c)) * TWELFTH)
                            diverge[key] = diverge[key] + grad[part, c] if key in diverge else grad[part, c]
                speed = {(part, d): load(vel(l, part, d)) for part in range(2) for d in dirs}
                for k in OWN:
                    m = k - l
                    if abs(m) > 2:
                        continue
                    a = abs(m)
                    for d in dirs:
                        gr, gi = grad[0, d], grad[1, d]
                        ur, ui = speed[0, d], speed[1, d]
                        fr, br = flow[a, 0, d], bend[a, 0, d]
                        add((k, 0), fr * gr + ur * br)
                        add((k, 1), fr * gi + ui * br)
                        if a:
                            fi, bi = flow[a, 1, d], bend[a, 1, d]
                            real, imag = fi * gi + ui * bi, fi * gr + ur * bi
                            (sub if m > 0 else add)((k, 0), real)
                            (add if m > 0 else sub)((k, 1), imag)
        for key, value in total.items():
            out[key[0], key[1], c, z, here, :] = value
    for (k, part), value in diverge.items():
        value = value * TWELFTH
        out[k, part, 3, z, here, :] = value if first else out[k, part, 3, z, here, :] + value


def kernel(pert, mean, modes, solid_hbm, out_hbm, own, low, high, flow, slabs, out, solid, local_sem, send_sem, recv_sem, out_sem):
    h, gx, gz = lax.axis_index("harm"), lax.axis_index("gx"), lax.axis_index("gz")
    side_x = {1: lax.rem(gx + 1, 4), -1: lax.rem(gx + 3, 4)}
    side_z = {1: lax.rem(gz + 1, 4), -1: lax.rem(gz + 3, 4)}
    odd = lax.rem(gz, 2)
    twin = {1: lax.rem(h + 4 * odd, 8), -1: lax.rem(h + 4 * (1 - odd), 8)}
    has_low, has_high = h > 0, h < 7

    barrier = pltpu.get_barrier_semaphore()

    def greet(device):
        pl.semaphore_signal(barrier, inc=1, device_id=device, device_id_type=MESH)

    for s in (1, -1):
        greet((h, side_x[s], gz))
        greet((h, gx, side_z[s]))
    greet((lax.rem(h + 4, 8), gx, 3 - gz))

    bent, across = odd == 1, lax.rem(gz + 2, 4)
    inner = jnp.logical_or(h == 3, h == 4)
    outer = jnp.logical_or(h == 0, h == 7)

    @pl.when(bent & inner)
    def _():
        greet((0, gx, across))
        greet((7, gx, across))

    @pl.when(bent & outer)
    def _():
        greet((3, gx, across))
        greet((4, gx, across))

    @pl.when(has_low)
    def _():
        greet((h - 1, gx, gz))

    @pl.when(has_high)
    def _():
        greet((h + 1, gx, gz))

    def local(i, src, dst):
        return pltpu.make_async_copy(src, dst, local_sem.at[i])

    loads = [
        local(0, pert, own.at[:, :, :, OWN_Z, OWN_X]),
        local(1, mean, flow.at[pl.ds(0, 3), OWN_Z, OWN_X]),
        local(2, modes.at[0, 0], flow.at[pl.ds(3, 3), OWN_Z, OWN_X]),
        local(3, modes.at[0, 1], flow.at[pl.ds(6, 3), OWN_Z, OWN_X]),
        local(4, modes.at[1, 0], flow.at[pl.ds(9, 3), OWN_Z, OWN_X]),
        local(5, modes.at[1, 1], flow.at[pl.ds(12, 3), OWN_Z, OWN_X]),
        local(6, solid_hbm, solid),
    ]
    for copy in loads:
        copy.start()

    extra = jnp.where(bent & jnp.logical_or(inner, outer), 2, 0)
    pl.semaphore_wait(barrier, 5 + jnp.where(has_low, 1, 0) + jnp.where(has_high, 1, 0) + extra)

    counter = iter(range(64))

    def remote(src, dst, device):
        i = next(counter)
        return pltpu.make_async_remote_copy(
            src_ref=src, dst_ref=dst, send_sem=send_sem.at[i], recv_sem=recv_sem.at[i], device_id=device, device_id_type=MESH
        )

    def again(i, src, dst, device):
        return pltpu.make_async_remote_copy(
            src_ref=src, dst_ref=dst, send_sem=send_sem.at[i], recv_sem=recv_sem.at[i], device_id=device, device_id_type=MESH
        )

    three = pl.ds(0, 3)

    def tile(j):
        return (pl.ds(j, 1), slice(None), slice(None), OWN_Z, OWN_X)

    turn_up, turn_down = bent & (h == 3), bent & (h == 4)
    pass_up, pass_down = bent & (h == 7), bent & (h == 0)
    up, down, leg_up, leg_down, on_up, on_down = [], [], [], [], [], []
    for j in range(2):
        up.append(remote(pert.at[pl.ds(2 + j, 1), :, three], low.at[tile(j)], (jnp.minimum(h + 1, 7), gx, gz)))
        down.append(remote(pert.at[pl.ds(j, 1), :, three], high.at[tile(j)], (jnp.maximum(h - 1, 0), gx, gz)))
        leg_up.append(remote(pert.at[pl.ds(2 + j, 1), :, three], high.at[tile(j)], (7, gx, across)))
        leg_down.append(remote(pert.at[pl.ds(j, 1), :, three], low.at[tile(j)], (0, gx, across)))
        on_up.append(again(4 * j, high.at[tile(j)], low.at[tile(j)], (4, gx, across)))
        on_down.append(again(4 * j + 1, low.at[tile(j)], high.at[tile(j)], (3, gx, across)))
    rim_x, rim_z, base_x, base_z = [], [], [], []
    for s in (1, -1):
        rim_z.append(remote(pert.at[:, :, :, BARE_Z[s]], own.at[:, :, :, RIM_Z[s], OWN_X], (h, gx, side_z[s])))
        rim_x.append(remote(pert.at[:, :, :, :, BARE_X[s]], own.at[:, :, :, OWN_Z, RIM_X[s]], (h, side_x[s], gz)))
        pieces = [(mean, 0)] + [(modes.at[m, part], 3 + (m * 2 + part) * 3) for m in range(2) for part in range(2)]
        for ref, at in pieces:
            fields = pl.ds(at, 3)
            base_x.append(remote(ref.at[:, :, BARE_X[s]], flow.at[fields, OWN_Z, RIM_X[s]], (h, side_x[s], gz)))
            base_z.append(remote(ref.at[:, BARE_Z[s]], flow.at[fields, RIM_Z[s], OWN_X], (twin[s], gx, side_z[s])))
    def starts(copies):
        def run():
            for copy in copies:
                copy.start()

        return run

    def arrivals(copies):
        def run():
            for copy in copies:
                copy.wait_recv()

        return run

    def departures(copies):
        def run():
            for copy in copies:
                copy.wait_send()

        return run

    up_here, down_here = has_high & jnp.logical_not(turn_up), has_low & jnp.logical_not(turn_down)
    pl.when(up_here)(starts(up))
    pl.when(turn_up)(starts(leg_up))
    pl.when(down_here)(starts(down))
    pl.when(turn_down)(starts(leg_down))
    for copy in rim_x + rim_z + base_x + base_z:
        copy.start()

    near_x = {}
    for name, ref in (("low", low), ("high", high)):
        near_x[name] = [
            remote(ref.at[:, :, :, OWN_Z, SLAB_X[s]], ref.at[:, :, :, OWN_Z, RIM_X[s]], (h, side_x[s], gz)) for s in (1, -1)
        ]

    def beside(ref):
        return [remote(ref.at[:, :, :, SLAB_Z[s], OWN_X], ref.at[:, :, :, RIM_Z[s], OWN_X], (h, gx, side_z[s])) for s in (1, -1)]

    def onward(harmonics, ref, target):
        return [
            remote(own.at[harmonics, :, three, RIM_Z[s], OWN_X], ref.at[:, :, :, RIM_Z[s], OWN_X], (target, gx, gz)) for s in (1, -1)
        ]

    lower = h < 4
    upper = jnp.logical_not(lower)
    high_x, low_x = beside(high), beside(low)
    low_y = onward(pl.ds(2, 2), low, jnp.minimum(h + 1, 7))
    high_y = onward(pl.ds(0, 2), high, jnp.maximum(h - 1, 0))
    corners = [(high_x, lower, lower), (low_x, upper, upper), (low_y, h < 3, lower & has_low), (high_y, h > 4, upper & has_high)]

    def stage(ref, shape, first, layers, rows, scale=None):
        def body(i, carry):
            index, rest = [], i
            for size in reversed(shape):
                index.insert(0, lax.rem(rest, size))
                rest = lax.div(rest, size)
            for z in layers:
                value = ref[(*index, z, rows)].astype(jnp.float32)
                slabs[first + i, z, rows, :] = value if scale is None else value * scale
            return carry

        count = 1
        for size in shape:
            count *= size
        lax.fori_loop(0, count, body, 0)

    middle, edge = range(2, 8), (0, 1, 8, 9)
    every = pl.ds(0, ROWS)
    for copy in loads:
        copy.wait()
    for copy in rim_x + base_x:
        copy.wait_recv()
    stage(own, (4, 2, 4), OWN0, middle, every)
    stage(flow, (15,), BASE0, middle, every, TWELFTH)

    lanes = lax.broadcasted_iota(jnp.int32, (8, LANES), 1)
    masks = {1: lanes < LANES - 1, 2: lanes < LANES - 2, -1: lanes >= 1, -2: lanes >= 2}
    freqs = [FREQUENCY_STEP * (h * 4 + k - 16).astype(jnp.float32) for k in range(4)]

    def sweep(jobs, first, finish=None):
        def layer(z, carry):
            def chunk(xb, inner):
                block(slabs, solid, out, masks, freqs, z, xb, jobs, first)
                return inner

            lax.fori_loop(0, 4, chunk, 0)
            if finish is not None:
                finish(z)
            return carry

        lax.fori_loop(0, 6, layer, 0)

    def pass_on(z):
        for j in range(2):
            for present, leg, second in ((pass_up, leg_up, on_up), (pass_down, leg_down, on_down)):

                @pl.when(present & (z == 2 + 2 * j))
                def _(leg=leg[j], second=second[j]):
                    leg.wait_recv()
                    second.start()

    sweep([(OWN, (0, 1))], True, pass_on)
    for copy in rim_z + base_z:
        copy.wait_recv()
    pl.when(h < 3)(starts(low_y))
    pl.when(h > 4)(starts(high_y))
    stage(own, (4, 2, 4), OWN0, edge, OWN_X)
    stage(flow, (15,), BASE0, edge, OWN_X, TWELFTH)

    def spread(z):
        for present, copies, name, half, beside_z in ((has_low, up, "low", upper, low_x), (has_high, down, "high", lower, high_x)):

            @pl.when(present & (z == 2))
            def _(copies=copies, name=name):
                arrivals(copies)()
                starts(near_x[name])()

            pl.when(half & (z == 2))(starts(beside_z))

    sweep([(OWN, (2,))], False, spread)

    def settle(present, ref, name, first):
        @pl.when(present)
        def _():
            arrivals(near_x[name])()
            stage(ref, (2, 2, 3), first, middle, every)

        @pl.when(jnp.logical_not(present))
        def _():
            def clear(i, carry):
                slabs[first + i] = jnp.zeros((LAYERS, ROWS, LANES), jnp.float32)
                return carry

            lax.fori_loop(0, 12, clear, 0)

    settle(has_low, low, "low", LOW0)
    settle(has_high, high, "high", HIGH0)
    sweep([(OTHERS, (0, 1))], False)
    for copies, _, comes in corners:
        pl.when(comes)(arrivals(copies))
    for present, ref, first in ((has_low, low, LOW0), (has_high, high, HIGH0)):

        @pl.when(present)
        def _(ref=ref, first=first):
            stage(ref, (2, 2, 3), first, edge, OWN_X)

    def write(z):
        return pltpu.make_async_copy(out.at[:, :, :, z], out_hbm.at[:, :, :, z], out_sem.at[z])

    sweep([(OTHERS, (2,))], False, lambda z: write(z).start())

    def drain(z, carry):
        write(z).wait()
        return carry

    lax.fori_loop(0, 6, drain, 0)
    for copy in rim_x + rim_z + base_x + base_z:
        copy.wait_send()
    pl.when(up_here)(departures(up))
    pl.when(turn_up)(departures(leg_up))
    pl.when(pass_up)(departures(on_up))
    pl.when(down_here)(departures(down))
    pl.when(turn_down)(departures(leg_down))
    pl.when(pass_down)(departures(on_down))
    pl.when(has_low)(departures(near_x["low"]))
    pl.when(has_high)(departures(near_x["high"]))
    for copies, goes, _ in corners:
        pl.when(goes)(departures(copies))


def shards(perturbation, base_mean, base_modes, solid_mask):
    turned = jnp.transpose(perturbation, (0, 1, 2, 4, 3, 5))
    mean = jnp.transpose(base_mean, (0, 2, 1, 3))
    modes = jnp.transpose(base_modes, (0, 1, 2, 4, 3, 5))
    mask = jnp.transpose(solid_mask, (1, 0, 2))
    anywhere = pl.BlockSpec(memory_space=pl.ANY)
    half = jnp.bfloat16
    out = pl.pallas_call(
        kernel,
        out_shape=jax.ShapeDtypeStruct(turned.shape, jnp.float32),
        in_specs=[anywhere] * 4,
        out_specs=anywhere,
        scratch_shapes=[
            pltpu.VMEM((4, 2, 4, LAYERS, ROWS, LANES), half),
            pltpu.VMEM((2, 2, 3, LAYERS, ROWS, LANES), half),
            pltpu.VMEM((2, 2, 3, LAYERS, ROWS, LANES), half),
            pltpu.VMEM((15, LAYERS, ROWS, LANES), half),
            pltpu.VMEM((FIELDS, LAYERS, ROWS, LANES), jnp.float32),
            pltpu.VMEM(turned.shape, jnp.float32),
            pltpu.VMEM(mask.shape, jnp.int32),
            pltpu.SemaphoreType.DMA((7,)),
            pltpu.SemaphoreType.DMA((44,)),
            pltpu.SemaphoreType.DMA((44,)),
            pltpu.SemaphoreType.DMA((6,)),
        ],
        compiler_params=pltpu.CompilerParams(collective_id=0, has_side_effects=True, vmem_limit_bytes=60 * 1024 * 1024),
    )(turned, mean, modes, mask)
    return jnp.transpose(out, (0, 1, 2, 4, 3, 5))


def solution(mesh):
    return jax.shard_map(
        shards,
        mesh=mesh,
        in_specs=(
            P("harm", None, None, "gx", "gz", None),
            P(None, "gx", "gz", None),
            P(None, None, None, "gx", "gz", None),
            P("gx", "gz", None),
        ),
        out_specs=P("harm", None, None, "gx", "gz", None),
        check_vma=False,
    )
```

```python
import jax
import jax.numpy as jnp
from jax import lax
from jax.experimental import pallas as pl
from jax.experimental.pallas import tpu as pltpu
from jax.sharding import PartitionSpec as P

FREQUENCY_STEP = 0.2
VISCOSITY = 0.05
PENALTY = 4.0
TWELFTH = 1.0 / 12.0
MESH = pl.DeviceIdType.MESH

LAYERS, ROWS, LANES = 10, 48, 128
SEMAPHORES = 48
OWN_Z = pl.ds(2, 6)
OWN_X = pl.ds(8, 32)
RIM_X = {1: pl.ds(6, 2), -1: pl.ds(40, 2)}
BARE_X = {1: pl.ds(30, 2), -1: pl.ds(0, 2)}

OWN0, LOW0, HIGH0, BASE0, FIELDS = 0, 32, 44, 56, 71


def vel(l, part, c):
    if l < 0:
        return LOW0 + ((l + 2) * 2 + part) * 3 + c
    if l > 3:
        return HIGH0 + ((l - 4) * 2 + part) * 3 + c
    return OWN0 + (l * 2 + part) * 4 + c


def base(m, part, c):
    return BASE0 + (c if m == 0 else 3 + ((m - 1) * 2 + part) * 3 + c)


MODES = [(0, 0), (1, 0), (1, 1), (2, 0), (2, 1)]
OWN = (0, 1, 2, 3)
OTHERS = (-2, -1, 4, 5)


def block(slabs, mask, out, masks, freqs, z, xb, jobs, first):
    row = xb * 8 + 8
    here = pl.ds(xb * 8, 8)

    def load(field, dz=0, dx=0):
        return slabs[field, z + 2 + dz, pl.ds(row + dx, 8), :]

    def lane(value, offset):
        return jnp.where(masks[offset], pltpu.roll(value, (-offset) % LANES, 1), 0.0)

    def sides(field, d):
        if d == 0:
            return tuple(load(field, 0, o) for o in (1, -1, 2, -2))
        if d == 2:
            return tuple(load(field, o, 0) for o in (1, -1, 2, -2))
        value = load(field)
        return tuple(lane(value, o) for o in (1, -1, 2, -2))

    def slope(s):
        return 8.0 * (s[0] - s[1]) - (s[2] - s[3])

    used = sorted({d for _, dirs in jobs for d in dirs})
    flow = {(m, part, d): load(base(m, part, d)) for m, part in MODES for d in used}
    solid = PENALTY * mask[z, here, :].astype(jnp.float32) if first else None
    diverge = {}
    for c in range(3):
        bend = {(m, part, d): slope(sides(base(m, part, c), d)) for m, part in MODES for d in used}
        total = {}
        if not first:
            total = {(k, part): out[k, part, c, z, here, :] for k in OWN for part in range(2)}

        def add(key, term):
            total[key] = total[key] + term if key in total else term

        def sub(key, term):
            total[key] = total[key] - term if key in total else -term

        for ls, dirs in jobs:
            for l in ls:
                grad = {}
                for part in range(2):
                    around = {d: sides(vel(l, part, c), d) for d in dirs}
                    for d in dirs:
                        grad[part, d] = slope(around[d])
                    if l in OWN:
                        key = (l, part)
                        near = sum(around[d][0] + around[d][1] for d in dirs)
                        far = sum(around[d][2] + around[d][3] for d in dirs)
                        sub(key, (VISCOSITY * 16.0 * TWELFTH) * near)
                        add(key, (VISCOSITY * TWELFTH) * far)
                        if 0 in dirs:
                            value = load(vel(l, part, c))
                            add(key, (solid + VISCOSITY * 90.0 * TWELFTH) * value)
                            turn = freqs[l] * load(vel(l, 1 - part, c))
                            (sub if part == 0 else add)(key, turn)
                        if c in dirs:
                            add(key, slope(sides(OWN0 + (l * 2 + part) * 4 + 3, c)) * TWELFTH)
                            diverge[key] = diverge[key] + grad[part, c] if key in diverge else grad[part, c]
                speed = {(part, d): load(vel(l, part, d)) for part in range(2) for d in dirs}
                for k in OWN:
                    m = k - l
                    if abs(m) > 2:
                        continue
                    a = abs(m)
                    for d in dirs:
                        gr, gi = grad[0, d], grad[1, d]
                        ur, ui = speed[0, d], speed[1, d]
                        fr, br = flow[a, 0, d], bend[a, 0, d]
                        add((k, 0), fr * gr + ur * br)
                        add((k, 1), fr * gi + ui * br)
                        if a:
                            fi, bi = flow[a, 1, d], bend[a, 1, d]
                            real, imag = fi * gi + ui * bi, fi * gr + ur * bi
                            (sub if m > 0 else add)((k, 0), real)
                            (add if m > 0 else sub)((k, 1), imag)
        for key, value in total.items():
            out[key[0], key[1], c, z, here, :] = value
    for (k, part), value in diverge.items():
        value = value * TWELFTH
        out[k, part, 3, z, here, :] = value if first else out[k, part, 3, z, here, :] + value


def kernel(pert, mean, modes, solid_hbm, out, own, low, high, flow, slabs, passing, solid, local_sem, send_sem, recv_sem):
    h, gx, gz = lax.axis_index("harm"), lax.axis_index("gx"), lax.axis_index("gz")
    side_x = {1: lax.rem(gx + 1, 4), -1: lax.rem(gx + 3, 4)}
    side_z = {1: lax.rem(gz + 1, 4), -1: lax.rem(gz + 3, 4)}
    odd = lax.rem(gz, 2)
    has_low, has_high = h > 0, h < 7

    barrier = pltpu.get_barrier_semaphore()

    def greet(device):
        pl.semaphore_signal(barrier, inc=1, device_id=device, device_id_type=MESH)

    for s in (1, -1):
        greet((h, side_x[s], gz))
        greet((h, gx, side_z[s]))
    greet((lax.rem(h + 4, 8), gx, 3 - gz))

    inner = jnp.logical_or(h == 3, h == 4)
    outer = jnp.logical_or(h == 0, h == 7)

    @pl.when(inner)
    def _():
        greet((7 - h, gx, 3 - gz))

    fellow = jnp.where(inner, 7 * lax.div(h, 4), 3 + lax.div(h, 4))

    @pl.when(jnp.logical_or(inner, outer))
    def _():
        greet((fellow, gx, gz))
        greet((fellow, gx, 3 - gz))

    @pl.when(has_low)
    def _():
        greet((h - 1, gx, gz))

    @pl.when(has_high)
    def _():
        greet((h + 1, gx, gz))

    def local(i, src, dst):
        return pltpu.make_async_copy(src, dst, local_sem.at[i])

    loads = [
        local(0, pert, own.at[:, :, :, OWN_Z, OWN_X]),
        local(1, mean, flow.at[pl.ds(0, 3), OWN_Z, OWN_X]),
        local(2, modes.at[0, 0], flow.at[pl.ds(3, 3), OWN_Z, OWN_X]),
        local(3, modes.at[0, 1], flow.at[pl.ds(6, 3), OWN_Z, OWN_X]),
        local(4, modes.at[1, 0], flow.at[pl.ds(9, 3), OWN_Z, OWN_X]),
        local(5, modes.at[1, 1], flow.at[pl.ds(12, 3), OWN_Z, OWN_X]),
        local(6, solid_hbm, solid),
    ]
    for copy in loads:
        copy.start()

    extra = jnp.where(jnp.logical_or(inner, outer), 2, 0) + jnp.where(inner, 1, 0)
    pl.semaphore_wait(barrier, 5 + jnp.where(has_low, 1, 0) + jnp.where(has_high, 1, 0) + extra)

    counter, places = iter(range(SEMAPHORES)), {}

    def remote(src, dst, device):
        i = next(counter)
        copy = pltpu.make_async_remote_copy(
            src_ref=src, dst_ref=dst, send_sem=send_sem.at[i], recv_sem=recv_sem.at[i], device_id=device, device_id_type=MESH
        )
        places[id(copy)] = i
        return copy

    def onto(first, src, dst, device):
        return pltpu.make_async_remote_copy(
            src_ref=src,
            dst_ref=dst,
            send_sem=send_sem.at[next(counter)],
            recv_sem=recv_sem.at[places[id(first)]],
            device_id=device,
            device_id_type=MESH,
        )

    three = pl.ds(0, 3)

    up = remote(pert.at[pl.ds(2, 2), :, three], low.at[:, :, :, OWN_Z, OWN_X], (jnp.minimum(h + 1, 7), gx, gz))
    down = remote(pert.at[pl.ds(0, 2), :, three], high.at[:, :, :, OWN_Z, OWN_X], (jnp.maximum(h - 1, 0), gx, gz))
    rim_x, base_x, base_mate, base_off = [], [], [], []
    for s in (1, -1):
        rim_x.append(remote(pert.at[:, :, :, :, BARE_X[s]], own.at[:, :, :, OWN_Z, RIM_X[s]], (h, side_x[s], gz)))
        pieces = [(mean, 0)] + [(modes.at[m, part], 3 + (m * 2 + part) * 3) for m in range(2) for part in range(2)]
        for ref, at in pieces:
            fields = pl.ds(at, 3)
            base_x.append(remote(ref.at[:, :, BARE_X[s]], flow.at[fields, OWN_Z, RIM_X[s]], (h, side_x[s], gz)))
    off, far_off = 8 * odd, 8 * (1 - odd)
    mate = gz + 1 - 2 * odd
    to_mate, to_off = pl.ds(4 * (1 - odd), 2), pl.ds(4 * odd, 2)
    at_mate, at_off = pl.ds(8 * odd, 2), pl.ds(far_off, 2)
    rim_mate = remote(pert.at[:, :, :, to_mate], own.at[:, :, :, at_mate, OWN_X], (h, gx, mate))
    rim_off = [
        remote(pert.at[half, :, :, to_off], own.at[half, :, :, at_off, OWN_X], (h, gx, 3 - gz)) for half in (pl.ds(0, 2), pl.ds(2, 2))
    ]
    detour = remote(pert.at[pl.ds(2, 2), :, :, to_off], passing, (fellow, gx, gz))
    resume = onto(rim_off[1], passing, own.at[pl.ds(2, 2), :, :, at_off, OWN_X], (fellow, gx, 3 - gz))
    for ref, at in pieces:
        fields = pl.ds(at, 3)
        base_mate.append(remote(ref.at[:, to_mate], flow.at[fields, at_mate, OWN_X], (h, gx, mate)))
        base_off.append(remote(ref.at[:, to_off], flow.at[fields, at_off, OWN_X], (lax.rem(h + 4, 8), gx, 3 - gz)))

    def starts(copies):
        def run():
            for copy in copies:
                copy.start()

        return run

    def arrivals(copies):
        def run():
            for copy in copies:
                copy.wait_recv()

        return run

    def departures(copies):
        def run():
            for copy in copies:
                copy.wait_send()

        return run

    pl.when(has_high)(up.start)
    pl.when(has_low)(down.start)
    pl.when(inner)(detour.start)
    for copy in [*rim_x, *base_x, rim_mate, *base_mate]:
        copy.start()

    @pl.when(jnp.logical_not(inner))
    def _():
        starts(rim_off)()
        starts(base_off)()

    forward_x, forward_z, straight_z, beside_z, across_z = {}, {}, {}, {}, {}
    for name, ref, side in (("low", low, 1), ("high", high, -1)):
        harmonics = pl.ds(2, 2) if side == 1 else pl.ds(0, 2)
        target = jnp.clip(h + side, 0, 7)
        forward_x[name] = [
            remote(own.at[harmonics, :, three, OWN_Z, RIM_X[s]], ref.at[:, :, :, OWN_Z, RIM_X[s]], (target, gx, gz)) for s in (1, -1)
        ]
        rim = pl.ds(off, 2)
        forward_z[name] = remote(own.at[harmonics, :, three, rim, OWN_X], ref.at[:, :, :, rim, OWN_X], (target, gx, gz))
        straight_z[name] = onto(
            forward_z[name], pert.at[harmonics, :, three, to_off], ref.at[:, :, :, at_off, OWN_X], (target, gx, 3 - gz)
        )
        across_z[name] = onto(
            forward_z[name], ref.at[:, :, :, pl.ds(2 + 4 * odd, 2), OWN_X], ref.at[:, :, :, at_off, OWN_X], (h, gx, 3 - gz)
        )
        beside_z[name] = remote(
            ref.at[:, :, :, pl.ds(6 - 4 * odd, 2), OWN_X], ref.at[:, :, :, at_mate, OWN_X], (h, gx, mate)
        )
    cross_up, cross_down = h == 3, h == 4
    onward_up, onward_down = has_high & jnp.logical_not(inner), has_low & jnp.logical_not(inner)

    def stage(ref, shape, first, layers, rows, scale=None):
        def body(i, carry):
            index, rest = [], i
            for size in reversed(shape):
                index.insert(0, lax.rem(rest, size))
                rest = lax.div(rest, size)
            for z in layers:
                value = ref[(*index, z, rows)].astype(jnp.float32)
                slabs[first + i, z, rows, :] = value if scale is None else value * scale
            return carry

        count = 1
        for size in shape:
            count *= size
        lax.fori_loop(0, count, body, 0)

    middle, edge = range(2, 8), (0, 1, 8, 9)
    every = pl.ds(0, ROWS)
    for copy in loads:
        copy.wait()
    for copy in rim_x:
        copy.wait_recv()
    pl.when(has_high)(starts(forward_x["low"]))
    pl.when(has_low)(starts(forward_x["high"]))
    pl.when(inner)(rim_off[0].start)
    arrivals(base_x)()
    stage(own, (4, 2, 4), OWN0, middle, every)
    stage(flow, (15,), BASE0, middle, every, TWELFTH)

    lanes = lax.broadcasted_iota(jnp.int32, (8, LANES), 1)
    masks = {1: lanes < LANES - 1, 2: lanes < LANES - 2, -1: lanes >= 1, -2: lanes >= 2}
    freqs = [FREQUENCY_STEP * (h * 4 + k - 16).astype(jnp.float32) for k in range(4)]

    def sweep(jobs, first, finish=None):
        def layer(z, carry):
            def chunk(xb, inner):
                block(slabs, solid, out, masks, freqs, z, xb, jobs, first)
                return inner

            lax.fori_loop(0, 4, chunk, 0)
            if finish is not None:
                finish(z)
            return carry

        lax.fori_loop(0, 6, layer, 0)

    def pass_on(z):
        @pl.when(outer & (z == 4))
        def _():
            detour.wait_recv()
            resume.start()

    sweep([(OWN, (0, 1))], True, pass_on)

    @pl.when(inner)
    def _():
        starts(base_off)()
        pl.when(cross_up)(straight_z["low"].start)
        pl.when(cross_down)(straight_z["high"].start)

    def own_rims():
        arrivals([rim_mate, *rim_off])()
        pl.when(onward_up)(forward_z["low"].start)
        pl.when(onward_down)(forward_z["high"].start)

    def neighbours():
        for present, copy, name, there in ((has_low, up, "low", h == 5), (has_high, down, "high", h == 2)):

            @pl.when(present)
            def _(copy=copy, name=name):
                copy.wait_recv()
                beside_z[name].start()

            pl.when(there)(across_z[name].start)

    def settle(present, ref, name, first):
        @pl.when(present)
        def _():
            arrivals(forward_x[name])()
            stage(ref, (2, 2, 3), first, middle, every)

        @pl.when(jnp.logical_not(present))
        def _():
            def clear(i, carry):
                slabs[first + i] = jnp.zeros((LAYERS, ROWS, LANES), jnp.float32)
                return carry

            lax.fori_loop(0, 12, clear, 0)

    def others():
        settle(has_low, low, "low", LOW0)
        settle(has_high, high, "high", HIGH0)
        sweep([(OTHERS, (0, 1))], False)

    late = jnp.logical_or(inner, outer)
    pl.when(jnp.logical_not(inner))(own_rims)

    @pl.when(late)
    def _():
        neighbours()
        others()

    pl.when(inner)(own_rims)
    arrivals(base_mate + base_off)()
    stage(own, (4, 2, 4), OWN0, edge, OWN_X)
    stage(flow, (15,), BASE0, edge, OWN_X, TWELFTH)

    def spread(z):
        pl.when(jnp.logical_not(late) & (z == 2))(neighbours)

    sweep([(OWN, (2,))], False, spread)
    pl.when(jnp.logical_not(late))(others)
    for present, ref, name, first in ((has_low, low, "low", LOW0), (has_high, high, "high", HIGH0)):

        @pl.when(present)
        def _(ref=ref, name=name, first=first):
            forward_z[name].wait_recv()
            beside_z[name].wait_recv()
            stage(ref, (2, 2, 3), first, edge, OWN_X)

    sweep([(OTHERS, (2,))], False)
    departures([*rim_x, *base_x, rim_mate, rim_off[0], *base_mate, *base_off])()
    pl.when(jnp.logical_not(inner))(rim_off[1].wait_send)
    pl.when(inner)(detour.wait_send)
    pl.when(outer)(resume.wait_send)
    pl.when(has_high)(up.wait_send)
    pl.when(has_low)(down.wait_send)
    for goes, onward, name in ((has_high, onward_up, "low"), (has_low, onward_down, "high")):
        pl.when(goes)(departures(forward_x[name]))
        pl.when(onward)(forward_z[name].wait_send)
    pl.when(cross_up)(straight_z["low"].wait_send)
    pl.when(cross_down)(straight_z["high"].wait_send)
    pl.when(h == 5)(across_z["low"].wait_send)
    pl.when(h == 2)(across_z["high"].wait_send)
    for present, name in ((has_low, "low"), (has_high, "high")):
        pl.when(present)(beside_z[name].wait_send)


def shards(perturbation, base_mean, base_modes, solid_mask):
    turned = jnp.transpose(perturbation, (0, 1, 2, 4, 3, 5))
    mean = jnp.transpose(base_mean, (0, 2, 1, 3))
    modes = jnp.transpose(base_modes, (0, 1, 2, 4, 3, 5))
    mask = jnp.transpose(solid_mask, (1, 0, 2))
    anywhere = pl.BlockSpec(memory_space=pl.ANY)
    vmem = pl.BlockSpec(memory_space=pltpu.VMEM)
    half = jnp.bfloat16
    out = pl.pallas_call(
        kernel,
        out_shape=jax.ShapeDtypeStruct(turned.shape, jnp.float32),
        in_specs=[anywhere] * 4,
        out_specs=vmem,
        scratch_shapes=[
            pltpu.VMEM((4, 2, 4, LAYERS, ROWS, LANES), half),
            pltpu.VMEM((2, 2, 3, LAYERS, ROWS, LANES), half),
            pltpu.VMEM((2, 2, 3, LAYERS, ROWS, LANES), half),
            pltpu.VMEM((15, LAYERS, ROWS, LANES), half),
            pltpu.VMEM((FIELDS, LAYERS, ROWS, LANES), jnp.float32),
            pltpu.VMEM((2, 2, 4, 2, 32, LANES), half),
            pltpu.VMEM(mask.shape, jnp.int32),
            pltpu.SemaphoreType.DMA((7,)),
            pltpu.SemaphoreType.DMA((SEMAPHORES,)),
            pltpu.SemaphoreType.DMA((SEMAPHORES,)),
        ],
        compiler_params=pltpu.CompilerParams(collective_id=0, has_side_effects=True, vmem_limit_bytes=36 * 1024 * 1024),
    )(*(pltpu.with_memory_space_constraint(array, pltpu.MemorySpace.HBM) for array in (turned, mean, modes, mask)))
    return jnp.transpose(out, (0, 1, 2, 4, 3, 5))


def solution(mesh):
    return jax.shard_map(
        shards,
        mesh=mesh,
        in_specs=(
            P("harm", None, None, "gx", "gz", None),
            P(None, "gx", "gz", None),
            P(None, None, None, "gx", "gz", None),
            P("gx", "gz", None),
        ),
        out_specs=P("harm", None, None, "gx", "gz", None),
        check_vma=False,
    )
```

```python
import jax
import jax.numpy as jnp
from jax import lax
from jax.experimental import pallas as pl
from jax.experimental.pallas import tpu as pltpu
from jax.sharding import PartitionSpec as P

FREQUENCY_STEP = 0.2
VISCOSITY = 0.05
PENALTY = 4.0
TWELFTH = 1.0 / 12.0
MESH = pl.DeviceIdType.MESH

LAYERS, ROWS, LANES = 10, 48, 128
SEMAPHORES = 56
OWN_BASE = 2
OWN_Z = pl.ds(2, 6)
OWN_X = pl.ds(8, 32)
RIM_X = {1: pl.ds(6, 2), -1: pl.ds(40, 2)}
BARE_X = {1: pl.ds(30, 2), -1: pl.ds(0, 2)}

OWN0, LOW0, HIGH0, BASE0, FIELDS = 0, 32, 44, 56, 71


def vel(l, part, c):
    if l < 0:
        return LOW0 + ((l + 2) * 2 + part) * 3 + c
    if l > 3:
        return HIGH0 + ((l - 4) * 2 + part) * 3 + c
    return OWN0 + (l * 2 + part) * 4 + c


def base(m, part, c):
    return BASE0 + (c if m == 0 else 3 + ((m - 1) * 2 + part) * 3 + c)


MODES = [(0, 0), (1, 0), (1, 1), (2, 0), (2, 1)]
OWN = (0, 1, 2, 3)
OTHERS = (-2, -1, 4, 5)


def block(slabs, slopes, bends, mask, out, freqs, z, xb, jobs, first):
    row = xb * 8 + 8
    here = pl.ds(xb * 8, 8)

    def load(field, dz=0, dx=0):
        return slabs[field, z + 2 + dz, pl.ds(row + dx, 8), :]

    def sides(field, d):
        if d == 0:
            return tuple(load(field, 0, o) for o in (1, -1, 2, -2))
        return tuple(load(field, o, 0) for o in (1, -1, 2, -2))

    def slope(s):
        return 8.0 * (s[0] - s[1]) - (s[2] - s[3])

    def along(field, d):
        return slopes[field, z, here, :] if d == 1 else slope(sides(field, d))

    used = sorted({d for _, dirs in jobs for d in dirs})
    flow = {(m, part, d): load(base(m, part, d)) for m, part in MODES for d in used}
    solid = PENALTY * mask[z, here, :].astype(jnp.float32) if first else None
    diverge = {}
    for c in range(3):
        bend = {(m, part, d): along(base(m, part, c), d) for m, part in MODES for d in used}
        total = {}
        if not first:
            total = {(k, part): out[2 * k + part, c, z, here, :] for k in OWN for part in range(2)}

        def add(key, term):
            total[key] = total[key] + term if key in total else term

        def sub(key, term):
            total[key] = total[key] - term if key in total else -term

        for ls, dirs in jobs:
            for l in ls:
                grad = {}
                for part in range(2):
                    around = {d: sides(vel(l, part, c), d) for d in dirs if d != 1}
                    for d in dirs:
                        grad[part, d] = slopes[vel(l, part, c), z, here, :] if d == 1 else slope(around[d])
                    if l in OWN:
                        key = (l, part)
                        near = sum(side[0] + side[1] for side in around.values())
                        far = sum(side[2] + side[3] for side in around.values())
                        bent = 16.0 * near - far
                        if 1 in dirs:
                            bent = bent + bends[vel(l, part, c), z, here, :]
                        sub(key, (VISCOSITY * TWELFTH) * bent)
                        if 0 in dirs:
                            value = load(vel(l, part, c))
                            add(key, (solid + VISCOSITY * 60.0 * TWELFTH) * value)
                            turn = freqs[l] * load(vel(l, 1 - part, c))
                            (sub if part == 0 else add)(key, turn)
                        if c in dirs:
                            add(key, along(OWN0 + (l * 2 + part) * 4 + 3, c) * TWELFTH)
                            diverge[key] = diverge[key] + grad[part, c] if key in diverge else grad[part, c]
                speed = {(part, d): load(vel(l, part, d)) for part in range(2) for d in dirs}
                for k in OWN:
                    m = k - l
                    if abs(m) > 2:
                        continue
                    a = abs(m)
                    for d in dirs:
                        gr, gi = grad[0, d], grad[1, d]
                        ur, ui = speed[0, d], speed[1, d]
                        fr, br = flow[a, 0, d], bend[a, 0, d]
                        add((k, 0), fr * gr + ur * br)
                        add((k, 1), fr * gi + ui * br)
                        if a:
                            fi, bi = flow[a, 1, d], bend[a, 1, d]
                            real, imag = fi * gi + ui * bi, fi * gr + ur * bi
                            (sub if m > 0 else add)((k, 0), real)
                            (add if m > 0 else sub)((k, 1), imag)
        for key, value in total.items():
            out[2 * key[0] + key[1], c, z, here, :] = value
    for (k, part), value in diverge.items():
        value = value * TWELFTH
        out[2 * k + part, 3, z, here, :] = value if first else out[2 * k + part, 3, z, here, :] + value


def kernel(pert, mean, modes, solid_hbm, out, own, low, high, flow, slabs, slopes, bends, band, passing, solid, local_sem, send_sem, recv_sem):
    h, gx, gz = lax.axis_index("harm"), lax.axis_index("gx"), lax.axis_index("gz")
    side_x = {1: lax.rem(gx + 1, 4), -1: lax.rem(gx + 3, 4)}
    side_z = {1: lax.rem(gz + 1, 4), -1: lax.rem(gz + 3, 4)}
    odd = lax.rem(gz, 2)
    has_low, has_high = h > 0, h < 7

    barrier = pltpu.get_barrier_semaphore()

    def greet(device):
        pl.semaphore_signal(barrier, inc=1, device_id=device, device_id_type=MESH)

    for s in (1, -1):
        greet((h, side_x[s], gz))
        greet((h, gx, side_z[s]))
    greet((lax.rem(h + 4, 8), gx, 3 - gz))

    inner = jnp.logical_or(h == 3, h == 4)
    outer = jnp.logical_or(h == 0, h == 7)

    @pl.when(inner)
    def _():
        greet((7 - h, gx, 3 - gz))

    fellow = jnp.where(inner, 7 * lax.div(h, 4), 3 + lax.div(h, 4))

    @pl.when(jnp.logical_or(inner, outer))
    def _():
        greet((fellow, gx, gz))
        greet((fellow, gx, 3 - gz))

    @pl.when(has_low)
    def _():
        greet((h - 1, gx, gz))

    @pl.when(has_high)
    def _():
        greet((h + 1, gx, gz))

    def local(i, src, dst):
        return pltpu.make_async_copy(src, dst, local_sem.at[i])

    loads = [
        local(0, pert, own.at[:, :, OWN_Z, OWN_X]),
        local(1, mean, flow.at[pl.ds(0, 3), OWN_Z, OWN_X]),
        local(2, modes, flow.at[pl.ds(3, 12), OWN_Z, OWN_X]),
        local(3, solid_hbm, solid),
    ]
    for copy in loads:
        copy.start()

    extra = jnp.where(jnp.logical_or(inner, outer), 2, 0) + jnp.where(inner, 1, 0)
    pl.semaphore_wait(barrier, 5 + jnp.where(has_low, 1, 0) + jnp.where(has_high, 1, 0) + extra)

    counter, places = iter(range(SEMAPHORES)), {}

    def remote(src, dst, device):
        i = next(counter)
        copy = pltpu.make_async_remote_copy(
            src_ref=src, dst_ref=dst, send_sem=send_sem.at[i], recv_sem=recv_sem.at[i], device_id=device, device_id_type=MESH
        )
        places[id(copy)] = i
        return copy

    def onto(first, src, dst, device):
        return pltpu.make_async_remote_copy(
            src_ref=src,
            dst_ref=dst,
            send_sem=send_sem.at[next(counter)],
            recv_sem=recv_sem.at[places[id(first)]],
            device_id=device,
            device_id_type=MESH,
        )

    three = pl.ds(0, 3)

    up = remote(pert.at[pl.ds(4, 4), three], low.at[:, :, OWN_Z, OWN_X], (jnp.minimum(h + 1, 7), gx, gz))
    down = remote(pert.at[pl.ds(0, 4), three], high.at[:, :, OWN_Z, OWN_X], (jnp.maximum(h - 1, 0), gx, gz))
    rim_x, base_x, base_mate, base_off, base_own = [], [], [], [], []
    for s in (1, -1):
        rim_x.append(remote(pert.at[:, :, :, BARE_X[s]], own.at[:, :, OWN_Z, RIM_X[s]], (h, side_x[s], gz)))
        for ref, at, count in ((mean, 0, 3), (modes, 3, 12)):
            base_x.append(remote(ref.at[:, :, BARE_X[s]], flow.at[pl.ds(at, count), OWN_Z, RIM_X[s]], (h, side_x[s], gz)))

    off, far_off = 8 * odd, 8 * (1 - odd)
    mate = gz + 1 - 2 * odd
    to_mate, to_off = pl.ds(4 * (1 - odd), 2), pl.ds(4 * odd, 2)
    at_mate, at_off = pl.ds(8 * odd, 2), pl.ds(far_off, 2)
    rim_mate = remote(pert.at[:, :, to_mate], own.at[:, :, at_mate, OWN_X], (h, gx, mate))
    rim_off = [
        remote(pert.at[half, :, to_off], own.at[half, :, at_off, OWN_X], (h, gx, 3 - gz)) for half in (pl.ds(0, 4), pl.ds(4, 4))
    ]
    detour = remote(pert.at[pl.ds(4, 4), :, to_off], passing, (fellow, gx, gz))
    resume = onto(rim_off[1], passing, own.at[pl.ds(4, 4), :, at_off, OWN_X], (fellow, gx, 3 - gz))
    for ref, start, at, count in ((mean, 0, 0, 3), (modes, 0, 3, 6), (modes, 6, 9, 6)):
        source, fields = ref.at[pl.ds(start, count)], pl.ds(at, count)
        base_mate.append(remote(source.at[:, to_mate], flow.at[fields, at_mate, OWN_X], (h, gx, mate)))
        base_off.append(remote(source.at[:, to_off], flow.at[fields, at_off, OWN_X], (lax.rem(h + 4, 8), gx, 3 - gz)))
        if len(base_own) < OWN_BASE:
            base_own.append(onto(base_off[-1], source.at[:, to_off], flow.at[fields, at_off, OWN_X], (h, gx, 3 - gz)))

    def starts(copies):
        def run():
            for copy in copies:
                copy.start()

        return run

    def arrivals(copies):
        def run():
            for copy in copies:
                copy.wait_recv()

        return run

    def departures(copies):
        def run():
            for copy in copies:
                copy.wait_send()

        return run

    pl.when(has_high)(up.start)
    pl.when(has_low)(down.start)
    pl.when(inner)(detour.start)
    for copy in [*rim_x, *base_x, rim_mate, *base_mate]:
        copy.start()

    @pl.when(jnp.logical_not(inner))
    def _():
        starts(rim_off)()
        starts(base_off)()

    pl.when(inner)(starts(base_off[OWN_BASE:]))

    forward_x, forward_z, straight_z, beside_z, across_z = {}, {}, {}, {}, {}
    for name, ref, side in (("low", low, 1), ("high", high, -1)):
        harmonics = pl.ds(4, 4) if side == 1 else pl.ds(0, 4)
        target = jnp.clip(h + side, 0, 7)
        forward_x[name] = [
            remote(own.at[harmonics, three, OWN_Z, RIM_X[s]], ref.at[:, :, OWN_Z, RIM_X[s]], (target, gx, gz)) for s in (1, -1)
        ]
        rim = pl.ds(off, 2)
        forward_z[name] = remote(own.at[harmonics, three, rim, OWN_X], ref.at[:, :, rim, OWN_X], (target, gx, gz))
        straight_z[name] = onto(
            forward_z[name], pert.at[harmonics, three, to_off], ref.at[:, :, at_off, OWN_X], (target, gx, 3 - gz)
        )
        across_z[name] = onto(
            forward_z[name], ref.at[:, :, pl.ds(2 + 4 * odd, 2), OWN_X], ref.at[:, :, at_off, OWN_X], (h, gx, 3 - gz)
        )
        beside_z[name] = remote(
            ref.at[:, :, pl.ds(6 - 4 * odd, 2), OWN_X], ref.at[:, :, at_mate, OWN_X], (h, gx, mate)
        )
    cross_up, cross_down = h == 3, h == 4
    pl.when(cross_up)(straight_z["low"].start)
    pl.when(cross_down)(straight_z["high"].start)
    onward_up, onward_down = has_high & jnp.logical_not(inner), has_low & jnp.logical_not(inner)

    def stage(ref, first, layers, rows, scale=None):
        groups, width = ref.shape[:2]

        def body(i, carry):
            for c in range(width):
                for z in layers:
                    for part in rows:
                        value = ref[i, c, z, part].astype(jnp.float32)
                        slabs[first + i * width + c, z, part, :] = value if scale is None else value * scale
            return carry

        lax.fori_loop(0, groups, body, 0)

    def stage_own(ref, first, curved, scale=None):
        groups, width = ref.shape[:2]
        weights = band[...] if curved else band[:, pl.ds(0, LANES)]

        def body(i, carry):
            fields = pl.ds(first + i * width, width)
            tile = ref[i, :, OWN_Z, OWN_X]
            value = tile.astype(jnp.float32)
            slabs[fields, OWN_Z, OWN_X, :] = value if scale is None else value * scale
            product = jnp.dot(tile.reshape(width * 192, LANES), weights, preferred_element_type=jnp.float32)
            if scale is not None:
                product = product * scale
            slopes[fields] = product[:, :LANES].reshape(width, 6, 32, LANES)
            if curved:
                bends[fields] = product[:, LANES:].reshape(width, 6, 32, LANES)
            return carry

        lax.fori_loop(0, groups, body, 0)

    middle = range(2, 8)
    flow_groups = flow.reshape(5, 3, LAYERS, ROWS, LANES)
    x_rims = (pl.ds(0, 8), pl.ds(40, 8))
    shift = lax.broadcasted_iota(jnp.int32, (LANES, LANES), 0) - lax.broadcasted_iota(jnp.int32, (LANES, LANES), 1)
    first_band, second_band = jnp.zeros((LANES, LANES), jnp.float32), jnp.zeros((LANES, LANES), jnp.float32)
    for offset, one, two in ((1, 8.0, 16.0), (-1, -8.0, 16.0), (2, -1.0, -1.0), (-2, 1.0, -1.0), (0, 0.0, -30.0)):
        first_band = jnp.where(shift == offset, one, first_band)
        second_band = jnp.where(shift == offset, two, second_band)
    band[:, pl.ds(0, LANES)] = first_band.astype(band.dtype)
    band[:, pl.ds(LANES, LANES)] = second_band.astype(band.dtype)
    for copy in loads:
        copy.wait()
    stage_own(own, OWN0, True)
    stage_own(flow_groups, BASE0, False, TWELFTH)

    freqs = [FREQUENCY_STEP * (h * 4 + k - 16).astype(jnp.float32) for k in range(4)]

    def sweep(jobs, first=False, layers=(0, 6), chunks=(0, 1, 4), finish=None):
        start, step, count = chunks

        def layer(j, carry):
            z = layers[0] + j

            def chunk(i, inner_carry):
                block(slabs, slopes, bends, solid, out, freqs, z, start + step * i, jobs, first)
                return inner_carry

            lax.fori_loop(0, count, chunk, 0)
            if finish is not None:
                finish(j)
            return carry

        lax.fori_loop(0, layers[1], layer, 0)

    free, bound = (2 - 2 * odd, 4), (4 * odd, 2)
    mate_edge, off_edge = [far_off, far_off + 1], [off, off + 1]

    sweep([(OWN, (0, 1))], True, chunks=(1, 1, 2))
    arrivals(rim_x)()
    pl.when(has_high)(starts(forward_x["low"]))
    pl.when(has_low)(starts(forward_x["high"]))
    pl.when(inner)(rim_off[0].start)
    arrivals(base_x)()
    stage(own, OWN0, middle, x_rims)
    stage(flow_groups, BASE0, middle, x_rims, TWELFTH)

    def pass_on(j):
        @pl.when(outer & (j == 2))
        def _():
            detour.wait_recv()
            resume.start()
            starts(base_own)()

    sweep([(OWN, (0, 1))], True, chunks=(0, 3, 2), finish=pass_on)
    arrivals([rim_mate, *base_mate])()
    stage(own, OWN0, mate_edge, (OWN_X,))
    stage(flow_groups, BASE0, mate_edge, (OWN_X,), TWELFTH)
    sweep([(OWN, (2,))], layers=free)

    @pl.when(jnp.logical_not(inner))
    def _():
        arrivals(rim_off)()
        pl.when(onward_up)(forward_z["low"].start)
        pl.when(onward_down)(forward_z["high"].start)

    def neighbours():
        for present, copy, name, there in ((has_low, up, "low", h == 5), (has_high, down, "high", h == 2)):

            @pl.when(present)
            def _(copy=copy, name=name):
                copy.wait_recv()
                beside_z[name].start()

            pl.when(there)(across_z[name].start)

    neighbours()
    for present, ref, name, first in ((has_low, low, "low", LOW0), (has_high, high, "high", HIGH0)):

        @pl.when(present)
        def _(ref=ref, name=name, first=first):
            stage_own(ref, first, False)
            arrivals(forward_x[name])()
            stage(ref, first, middle, x_rims)
            beside_z[name].wait_recv()
            stage(ref, first, mate_edge, (OWN_X,))

        @pl.when(jnp.logical_not(present))
        def _(first=first):
            def clear(i, carry):
                slabs[first + i] = jnp.zeros((LAYERS, ROWS, LANES), jnp.float32)
                slopes[first + i] = jnp.zeros((6, 32, LANES), jnp.float32)
                return carry

            lax.fori_loop(0, 12, clear, 0)

    sweep([(OTHERS, (0, 1, 2))], layers=free)
    sweep([(OTHERS, (0, 1))], layers=bound)
    pl.when(inner)(arrivals(rim_off))
    arrivals(base_off)()
    stage(own, OWN0, off_edge, (OWN_X,))
    stage(flow_groups, BASE0, off_edge, (OWN_X,), TWELFTH)
    for present, ref, name, first in ((has_low, low, "low", LOW0), (has_high, high, "high", HIGH0)):

        @pl.when(present)
        def _(ref=ref, name=name, first=first):
            forward_z[name].wait_recv()
            stage(ref, first, off_edge, (OWN_X,))

    sweep([(OWN, (2,)), (OTHERS, (2,))], layers=bound)
    departures([*rim_x, *base_x, rim_mate, rim_off[0], *base_mate])()
    pl.when(jnp.logical_not(inner))(departures([rim_off[1], *base_off[:OWN_BASE]]))
    departures(base_off[OWN_BASE:])()
    pl.when(outer)(departures(base_own))
    pl.when(inner)(detour.wait_send)
    pl.when(outer)(resume.wait_send)
    pl.when(has_high)(up.wait_send)
    pl.when(has_low)(down.wait_send)
    for goes, onward, name in ((has_high, onward_up, "low"), (has_low, onward_down, "high")):
        pl.when(goes)(departures(forward_x[name]))
        pl.when(onward)(forward_z[name].wait_send)
    pl.when(cross_up)(straight_z["low"].wait_send)
    pl.when(cross_down)(straight_z["high"].wait_send)
    pl.when(h == 5)(across_z["low"].wait_send)
    pl.when(h == 2)(across_z["high"].wait_send)
    for present, name in ((has_low, "low"), (has_high, "high")):
        pl.when(present)(beside_z[name].wait_send)


def shards(perturbation, base_mean, base_modes, solid_mask):
    per, _, _, cx, cz, cy = perturbation.shape
    turned = jnp.transpose(perturbation, (0, 1, 2, 4, 3, 5)).reshape(per * 2, 4, cz, cx, cy)
    mean = jnp.transpose(base_mean, (0, 2, 1, 3))
    modes = jnp.transpose(base_modes, (0, 1, 2, 4, 3, 5)).reshape(12, cz, cx, cy)
    mask = jnp.transpose(solid_mask, (1, 0, 2))
    anywhere = pl.BlockSpec(memory_space=pl.ANY)
    vmem = pl.BlockSpec(memory_space=pltpu.VMEM)
    half = jnp.bfloat16
    out = pl.pallas_call(
        kernel,
        out_shape=jax.ShapeDtypeStruct(turned.shape, jnp.float32),
        in_specs=[anywhere] * 4,
        out_specs=vmem,
        scratch_shapes=[
            pltpu.VMEM((8, 4, LAYERS, ROWS, LANES), half),
            pltpu.VMEM((4, 3, LAYERS, ROWS, LANES), half),
            pltpu.VMEM((4, 3, LAYERS, ROWS, LANES), half),
            pltpu.VMEM((15, LAYERS, ROWS, LANES), half),
            pltpu.VMEM((FIELDS, LAYERS, ROWS, LANES), jnp.float32),
            pltpu.VMEM((FIELDS, 6, 32, LANES), jnp.float32),
            pltpu.VMEM((32, 6, 32, LANES), jnp.float32),
            pltpu.VMEM((LANES, 2 * LANES), half),
            pltpu.VMEM((4, 4, 2, 32, LANES), half),
            pltpu.VMEM(mask.shape, jnp.int32),
            pltpu.SemaphoreType.DMA((4,)),
            pltpu.SemaphoreType.DMA((SEMAPHORES,)),
            pltpu.SemaphoreType.DMA((SEMAPHORES,)),
        ],
        compiler_params=pltpu.CompilerParams(collective_id=0, has_side_effects=True, vmem_limit_bytes=46 * 1024 * 1024),
    )(*(pltpu.with_memory_space_constraint(array, pltpu.MemorySpace.HBM) for array in (turned, mean, modes, mask)))
    return jnp.transpose(out.reshape(per, 2, 4, cz, cx, cy), (0, 1, 2, 4, 3, 5))


def solution(mesh):
    return jax.shard_map(
        shards,
        mesh=mesh,
        in_specs=(
            P("harm", None, None, "gx", "gz", None),
            P(None, "gx", "gz", None),
            P(None, None, None, "gx", "gz", None),
            P("gx", "gz", None),
        ),
        out_specs=P("harm", None, None, "gx", "gz", None),
        check_vma=False,
    )
```

```python
import jax
import jax.numpy as jnp
from jax import lax
from jax.experimental import pallas as pl
from jax.experimental.pallas import tpu as pltpu
from jax.sharding import PartitionSpec as P

FREQUENCY_STEP = 0.2
VISCOSITY = 0.05
PENALTY = 4.0
TWELFTH = 1.0 / 12.0
MESH = pl.DeviceIdType.MESH

LAYERS, ROWS, LANES = 10, 48, 128
SEMAPHORES = 56
OWN_Z = pl.ds(2, 6)
OWN_X = pl.ds(8, 32)
RIM_X = {1: pl.ds(6, 2), -1: pl.ds(40, 2)}
BARE_X = {1: pl.ds(30, 2), -1: pl.ds(0, 2)}

OWN0, LOW0, HIGH0, BASE0, FIELDS = 0, 32, 44, 56, 71


def vel(l, part, c):
    if l < 0:
        return LOW0 + ((l + 2) * 2 + part) * 3 + c
    if l > 3:
        return HIGH0 + ((l - 4) * 2 + part) * 3 + c
    return OWN0 + (l * 2 + part) * 4 + c


def base(m, part, c):
    return BASE0 + (c if m == 0 else 3 + ((m - 1) * 2 + part) * 3 + c)


MODES = [(0, 0), (1, 0), (1, 1), (2, 0), (2, 1)]
OWN = (0, 1, 2, 3)
OTHERS = (-2, -1, 4, 5)


def block(slabs, slopes, bends, mask, out, freqs, z, xb, jobs, first):
    row = xb * 8 + 8
    here = pl.ds(xb * 8, 8)

    def load(field, dz=0, dx=0):
        return slabs[field, z + 2 + dz, pl.ds(row + dx, 8), :]

    def sides(field, d):
        if d == 0:
            return tuple(load(field, 0, o) for o in (1, -1, 2, -2))
        return tuple(load(field, o, 0) for o in (1, -1, 2, -2))

    def slope(s):
        return 8.0 * (s[0] - s[1]) - (s[2] - s[3])

    def along(field, d):
        return slopes[field, z, here, :] if d == 1 else slope(sides(field, d))

    used = sorted({d for _, dirs in jobs for d in dirs})
    flow = {(m, part, d): load(base(m, part, d)) for m, part in MODES for d in used}
    solid = PENALTY * mask[z, here, :].astype(jnp.float32) if first else None
    diverge = {}
    for c in range(3):
        bend = {(m, part, d): along(base(m, part, c), d) for m, part in MODES for d in used}
        total = {}
        if not first:
            total = {(k, part): out[2 * k + part, c, z, here, :] for k in OWN for part in range(2)}

        def add(key, term):
            total[key] = total[key] + term if key in total else term

        def sub(key, term):
            total[key] = total[key] - term if key in total else -term

        for ls, dirs in jobs:
            for l in ls:
                grad = {}
                for part in range(2):
                    around = {d: sides(vel(l, part, c), d) for d in dirs if d != 1}
                    for d in dirs:
                        grad[part, d] = slopes[vel(l, part, c), z, here, :] if d == 1 else slope(around[d])
                    if l in OWN:
                        key = (l, part)
                        near = sum(side[0] + side[1] for side in around.values())
                        far = sum(side[2] + side[3] for side in around.values())
                        bent = 16.0 * near - far
                        if 1 in dirs:
                            bent = bent + bends[vel(l, part, c), z, here, :]
                        sub(key, (VISCOSITY * TWELFTH) * bent)
                        if 0 in dirs:
                            value = load(vel(l, part, c))
                            add(key, (solid + VISCOSITY * 60.0 * TWELFTH) * value)
                            turn = freqs[l] * load(vel(l, 1 - part, c))
                            (sub if part == 0 else add)(key, turn)
                        if c in dirs:
                            add(key, along(OWN0 + (l * 2 + part) * 4 + 3, c) * TWELFTH)
                            diverge[key] = diverge[key] + grad[part, c] if key in diverge else grad[part, c]
                speed = {(part, d): load(vel(l, part, d)) for part in range(2) for d in dirs}
                for k in OWN:
                    m = k - l
                    if abs(m) > 2:
                        continue
                    a = abs(m)
                    for d in dirs:
                        gr, gi = grad[0, d], grad[1, d]
                        ur, ui = speed[0, d], speed[1, d]
                        fr, br = flow[a, 0, d], bend[a, 0, d]
                        add((k, 0), fr * gr + ur * br)
                        add((k, 1), fr * gi + ui * br)
                        if a:
                            fi, bi = flow[a, 1, d], bend[a, 1, d]
                            real, imag = fi * gi + ui * bi, fi * gr + ur * bi
                            (sub if m > 0 else add)((k, 0), real)
                            (add if m > 0 else sub)((k, 1), imag)
        for key, value in total.items():
            out[2 * key[0] + key[1], c, z, here, :] = value
    for (k, part), value in diverge.items():
        value = value * TWELFTH
        out[2 * k + part, 3, z, here, :] = value if first else out[2 * k + part, 3, z, here, :] + value


def kernel(pert, mean, modes, solid_hbm, out, own, low, high, flow, slabs, slopes, bends, band, passing, solid, local_sem, send_sem, recv_sem):
    h, gx, gz = lax.axis_index("harm"), lax.axis_index("gx"), lax.axis_index("gz")
    side_x = {1: lax.rem(gx + 1, 4), -1: lax.rem(gx + 3, 4)}
    side_z = {1: lax.rem(gz + 1, 4), -1: lax.rem(gz + 3, 4)}
    odd = lax.rem(gz, 2)
    has_low, has_high = h > 0, h < 7

    barrier = pltpu.get_barrier_semaphore()

    def greet(device):
        pl.semaphore_signal(barrier, inc=1, device_id=device, device_id_type=MESH)

    for s in (1, -1):
        greet((h, side_x[s], gz))
        greet((h, gx, side_z[s]))
    greet((lax.rem(h + 4, 8), gx, 3 - gz))

    inner = jnp.logical_or(h == 3, h == 4)
    outer = jnp.logical_or(h == 0, h == 7)

    @pl.when(inner)
    def _():
        greet((7 - h, gx, 3 - gz))

    fellow = jnp.where(inner, 7 * lax.div(h, 4), 3 + lax.div(h, 4))

    @pl.when(jnp.logical_or(inner, outer))
    def _():
        greet((fellow, gx, gz))
        greet((lax.rem(h + 4, 8), gx, gz))

    @pl.when(has_low)
    def _():
        greet((h - 1, gx, gz))

    @pl.when(has_high)
    def _():
        greet((h + 1, gx, gz))

    def local(i, src, dst):
        return pltpu.make_async_copy(src, dst, local_sem.at[i])

    loads = [
        local(0, pert, own.at[:, :, OWN_Z, OWN_X]),
        local(1, mean, flow.at[pl.ds(0, 3), OWN_Z, OWN_X]),
        local(2, modes, flow.at[pl.ds(3, 12), OWN_Z, OWN_X]),
        local(3, solid_hbm, solid),
    ]
    for copy in loads:
        copy.start()

    extra = jnp.where(jnp.logical_or(inner, outer), 2, 0) + jnp.where(inner, 1, 0)
    pl.semaphore_wait(barrier, 5 + jnp.where(has_low, 1, 0) + jnp.where(has_high, 1, 0) + extra)

    counter, places = iter(range(SEMAPHORES)), {}

    def remote(src, dst, device):
        i = next(counter)
        copy = pltpu.make_async_remote_copy(
            src_ref=src, dst_ref=dst, send_sem=send_sem.at[i], recv_sem=recv_sem.at[i], device_id=device, device_id_type=MESH
        )
        places[id(copy)] = i
        return copy

    def onto(first, src, dst, device):
        return pltpu.make_async_remote_copy(
            src_ref=src,
            dst_ref=dst,
            send_sem=send_sem.at[next(counter)],
            recv_sem=recv_sem.at[places[id(first)]],
            device_id=device,
            device_id_type=MESH,
        )

    three = pl.ds(0, 3)

    up, down = [], []
    for j in range(2):
        part = pl.ds(2 * j, 2)
        up.append(remote(pert.at[pl.ds(4 + 2 * j, 2), three], low.at[part, :, OWN_Z, OWN_X], (jnp.minimum(h + 1, 7), gx, gz)))
        down.append(remote(pert.at[part, three], high.at[part, :, OWN_Z, OWN_X], (jnp.maximum(h - 1, 0), gx, gz)))
    detour, resume_up, resume_down = [], [], []
    for z in (0, 3):
        layers, inside = pl.ds(z, 3), pl.ds(2 + z, 3)
        detour.append(remote(pert.at[pl.ds(6 - 4 * lax.div(h, 4), 2), three, layers], passing.at[:, :, layers], (fellow, gx, gz)))
        resume_up.append(onto(up[1], passing.at[:, :, layers], low.at[pl.ds(2, 2), :, inside, OWN_X], (4, gx, gz)))
        resume_down.append(onto(down[1], passing.at[:, :, layers], high.at[pl.ds(2, 2), :, inside, OWN_X], (3, gx, gz)))
    rim_x, base_x, base_mate, base_off = [], [], [], []
    for s in (1, -1):
        rim_x.append(remote(pert.at[:, :, :, BARE_X[s]], own.at[:, :, OWN_Z, RIM_X[s]], (h, side_x[s], gz)))
        for ref, at, count in ((mean, 0, 3), (modes, 3, 12)):
            base_x.append(remote(ref.at[:, :, BARE_X[s]], flow.at[pl.ds(at, count), OWN_Z, RIM_X[s]], (h, side_x[s], gz)))

    off, far_off = 8 * odd, 8 * (1 - odd)
    mate = gz + 1 - 2 * odd
    to_mate, to_off = pl.ds(4 * (1 - odd), 2), pl.ds(4 * odd, 2)
    at_mate, at_off = pl.ds(8 * odd, 2), pl.ds(far_off, 2)
    rim_mate = remote(pert.at[:, :, to_mate], own.at[:, :, at_mate, OWN_X], (h, gx, mate))
    rim_off = [
        remote(pert.at[half, :, to_off], own.at[half, :, at_off, OWN_X], (h, gx, 3 - gz)) for half in (pl.ds(0, 4), pl.ds(4, 4))
    ]
    for ref, start, at, count in ((mean, 0, 0, 3), (modes, 0, 3, 6), (modes, 6, 9, 6)):
        source, fields = ref.at[pl.ds(start, count)], pl.ds(at, count)
        base_mate.append(remote(source.at[:, to_mate], flow.at[fields, at_mate, OWN_X], (h, gx, mate)))
        base_off.append(remote(source.at[:, to_off], flow.at[fields, at_off, OWN_X], (lax.rem(h + 4, 8), gx, 3 - gz)))

    def starts(copies):
        def run():
            for copy in copies:
                copy.start()

        return run

    def arrivals(copies):
        def run():
            for copy in copies:
                copy.wait_recv()

        return run

    def departures(copies):
        def run():
            for copy in copies:
                copy.wait_send()

        return run

    pl.when(inner)(starts(detour))
    pl.when(has_high)(up[0].start)
    pl.when(has_low)(down[0].start)
    cross_up, cross_down = h == 3, h == 4
    up_here, down_here = has_high & jnp.logical_not(cross_up), has_low & jnp.logical_not(cross_down)
    pl.when(up_here)(up[1].start)
    pl.when(down_here)(down[1].start)
    for copy in [*rim_x, *base_x, rim_mate, *base_mate]:
        copy.start()
    normal = jnp.logical_not(jnp.logical_or(inner, outer))
    pl.when(normal | (h == 7))(rim_off[0].start)
    pl.when(normal | (h == 0))(rim_off[1].start)
    for copy in base_off:
        copy.start()

    forward_x, forward_z, straight_z, beside_z, across_z = {}, {}, {}, {}, {}
    for name, ref, side in (("low", low, 1), ("high", high, -1)):
        harmonics = pl.ds(4, 4) if side == 1 else pl.ds(0, 4)
        target = jnp.clip(h + side, 0, 7)
        forward_x[name] = [
            remote(own.at[harmonics, three, OWN_Z, RIM_X[s]], ref.at[:, :, OWN_Z, RIM_X[s]], (target, gx, gz)) for s in (1, -1)
        ]
        rim = pl.ds(off, 2)
        forward_z[name] = remote(own.at[harmonics, three, rim, OWN_X], ref.at[:, :, rim, OWN_X], (target, gx, gz))
        straight_z[name] = onto(
            forward_z[name], pert.at[harmonics, three, to_off], ref.at[:, :, at_off, OWN_X], (target, gx, 3 - gz)
        )
        across_z[name] = onto(
            forward_z[name], ref.at[:, :, pl.ds(2 + 4 * odd, 2), OWN_X], ref.at[:, :, at_off, OWN_X], (h, gx, 3 - gz)
        )
        beside_z[name] = remote(
            ref.at[:, :, pl.ds(6 - 4 * odd, 2), OWN_X], ref.at[:, :, at_mate, OWN_X], (h, gx, mate)
        )
    pl.when(cross_up)(straight_z["low"].start)
    pl.when(cross_down)(straight_z["high"].start)
    onward_up, onward_down = has_high & jnp.logical_not(inner), has_low & jnp.logical_not(inner)

    def stage(ref, first, layers, rows, scale=None):
        groups, width = ref.shape[:2]

        def body(i, carry):
            for c in range(width):
                for z in layers:
                    for part in rows:
                        value = ref[i, c, z, part].astype(jnp.float32)
                        slabs[first + i * width + c, z, part, :] = value if scale is None else value * scale
            return carry

        lax.fori_loop(0, groups, body, 0)

    def stage_own(ref, first, curved, scale=None):
        groups, width = ref.shape[:2]
        weights = band[...] if curved else band[:, pl.ds(0, LANES)]

        def body(i, carry):
            fields = pl.ds(first + i * width, width)
            tile = ref[i, :, OWN_Z, OWN_X]
            value = tile.astype(jnp.float32)
            slabs[fields, OWN_Z, OWN_X, :] = value if scale is None else value * scale
            product = jnp.dot(tile.reshape(width * 192, LANES), weights, preferred_element_type=jnp.float32)
            if scale is not None:
                product = product * scale
            slopes[fields] = product[:, :LANES].reshape(width, 6, 32, LANES)
            if curved:
                bends[fields] = product[:, LANES:].reshape(width, 6, 32, LANES)
            return carry

        lax.fori_loop(0, groups, body, 0)

    middle = range(2, 8)
    flow_groups = flow.reshape(5, 3, LAYERS, ROWS, LANES)
    x_rims = (pl.ds(0, 8), pl.ds(40, 8))
    shift = lax.broadcasted_iota(jnp.int32, (LANES, LANES), 0) - lax.broadcasted_iota(jnp.int32, (LANES, LANES), 1)
    first_band, second_band = jnp.zeros((LANES, LANES), jnp.float32), jnp.zeros((LANES, LANES), jnp.float32)
    for offset, one, two in ((1, 8.0, 16.0), (-1, -8.0, 16.0), (2, -1.0, -1.0), (-2, 1.0, -1.0), (0, 0.0, -30.0)):
        first_band = jnp.where(shift == offset, one, first_band)
        second_band = jnp.where(shift == offset, two, second_band)
    band[:, pl.ds(0, LANES)] = first_band.astype(band.dtype)
    band[:, pl.ds(LANES, LANES)] = second_band.astype(band.dtype)
    for copy in loads:
        copy.wait()
    stage_own(own, OWN0, True)
    stage_own(flow_groups, BASE0, False, TWELFTH)

    freqs = [FREQUENCY_STEP * (h * 4 + k - 16).astype(jnp.float32) for k in range(4)]

    def sweep(jobs, first=False, layers=(0, 6), chunks=(0, 1, 4), finish=None):
        start, step, count = chunks

        def layer(j, carry):
            z = layers[0] + j

            def chunk(i, inner_carry):
                block(slabs, slopes, bends, solid, out, freqs, z, start + step * i, jobs, first)
                return inner_carry

            lax.fori_loop(0, count, chunk, 0)
            if finish is not None:
                finish(j)
            return carry

        lax.fori_loop(0, layers[1], layer, 0)

    free, bound = (2 - 2 * odd, 4), (4 * odd, 2)
    mate_edge, off_edge = [far_off, far_off + 1], [off, off + 1]

    def pass_half(i):
        detour[i].wait_recv()
        pl.when(h == 0)(resume_up[i].start)
        pl.when(h == 7)(resume_down[i].start)

    sweep([(OWN, (0, 1))], True, chunks=(1, 1, 2))

    @pl.when(outer)
    def _():
        pass_half(0)

    arrivals(rim_x)()
    pl.when(has_high)(starts(forward_x["low"]))
    pl.when(has_low)(starts(forward_x["high"]))
    pl.when(inner)(starts(rim_off))
    arrivals(base_x)()
    stage(own, OWN0, middle, x_rims)
    stage(flow_groups, BASE0, middle, x_rims, TWELFTH)

    def pass_on(j):
        @pl.when(outer & (j == 2))
        def _():
            pass_half(1)
            pl.when(h == 0)(rim_off[0].start)
            pl.when(h == 7)(rim_off[1].start)

    sweep([(OWN, (0, 1))], True, chunks=(0, 3, 2), finish=pass_on)
    arrivals([rim_mate, *base_mate])()
    stage(own, OWN0, mate_edge, (OWN_X,))
    stage(flow_groups, BASE0, mate_edge, (OWN_X,), TWELFTH)
    sweep([(OWN, (2,))], layers=free)

    @pl.when(jnp.logical_not(inner))
    def _():
        pl.when(h != 0)(rim_off[0].wait_recv)
        pl.when(h != 7)(rim_off[1].wait_recv)
        pl.when(onward_up)(forward_z["low"].start)
        pl.when(onward_down)(forward_z["high"].start)

    def neighbours():
        for present, copies, name, there in ((has_low, up, "low", h == 5), (has_high, down, "high", h == 2)):

            @pl.when(present)
            def _(copies=copies, name=name):
                arrivals(copies)()
                beside_z[name].start()

            pl.when(there)(across_z[name].start)

    neighbours()
    for present, ref, name, first in ((has_low, low, "low", LOW0), (has_high, high, "high", HIGH0)):

        @pl.when(present)
        def _(ref=ref, name=name, first=first):
            stage_own(ref, first, False)
            arrivals(forward_x[name])()
            stage(ref, first, middle, x_rims)
            beside_z[name].wait_recv()
            stage(ref, first, mate_edge, (OWN_X,))

        @pl.when(jnp.logical_not(present))
        def _(first=first):
            def clear(i, carry):
                slabs[first + i] = jnp.zeros((LAYERS, ROWS, LANES), jnp.float32)
                slopes[first + i] = jnp.zeros((6, 32, LANES), jnp.float32)
                return carry

            lax.fori_loop(0, 12, clear, 0)

    sweep([(OTHERS, (0, 1, 2))], layers=free)
    sweep([(OTHERS, (0, 1))], layers=bound)
    pl.when(inner | (h == 0))(rim_off[0].wait_recv)
    pl.when(inner | (h == 7))(rim_off[1].wait_recv)
    arrivals(base_off)()
    stage(own, OWN0, off_edge, (OWN_X,))
    stage(flow_groups, BASE0, off_edge, (OWN_X,), TWELFTH)
    for present, ref, name, first in ((has_low, low, "low", LOW0), (has_high, high, "high", HIGH0)):

        @pl.when(present)
        def _(ref=ref, name=name, first=first):
            forward_z[name].wait_recv()
            stage(ref, first, off_edge, (OWN_X,))

    sweep([(OWN, (2,)), (OTHERS, (2,))], layers=bound)
    departures([*rim_x, *base_x, rim_mate, *rim_off, *base_mate, *base_off])()
    pl.when(inner)(departures(detour))
    pl.when(h == 0)(departures(resume_up))
    pl.when(h == 7)(departures(resume_down))
    pl.when(has_high)(up[0].wait_send)
    pl.when(has_low)(down[0].wait_send)
    pl.when(up_here)(up[1].wait_send)
    pl.when(down_here)(down[1].wait_send)
    for goes, onward, name in ((has_high, onward_up, "low"), (has_low, onward_down, "high")):
        pl.when(goes)(departures(forward_x[name]))
        pl.when(onward)(forward_z[name].wait_send)
    pl.when(cross_up)(straight_z["low"].wait_send)
    pl.when(cross_down)(straight_z["high"].wait_send)
    pl.when(h == 5)(across_z["low"].wait_send)
    pl.when(h == 2)(across_z["high"].wait_send)
    for present, name in ((has_low, "low"), (has_high, "high")):
        pl.when(present)(beside_z[name].wait_send)


def shards(perturbation, base_mean, base_modes, solid_mask):
    per, _, _, cx, cz, cy = perturbation.shape
    turned = jnp.transpose(perturbation, (0, 1, 2, 4, 3, 5)).reshape(per * 2, 4, cz, cx, cy)
    mean = jnp.transpose(base_mean, (0, 2, 1, 3))
    modes = jnp.transpose(base_modes, (0, 1, 2, 4, 3, 5)).reshape(12, cz, cx, cy)
    mask = jnp.transpose(solid_mask, (1, 0, 2))
    anywhere = pl.BlockSpec(memory_space=pl.ANY)
    vmem = pl.BlockSpec(memory_space=pltpu.VMEM)
    half = jnp.bfloat16
    out = pl.pallas_call(
        kernel,
        out_shape=jax.ShapeDtypeStruct(turned.shape, jnp.float32),
        in_specs=[anywhere] * 4,
        out_specs=vmem,
        scratch_shapes=[
            pltpu.VMEM((8, 4, LAYERS, ROWS, LANES), half),
            pltpu.VMEM((4, 3, LAYERS, ROWS, LANES), half),
            pltpu.VMEM((4, 3, LAYERS, ROWS, LANES), half),
            pltpu.VMEM((15, LAYERS, ROWS, LANES), half),
            pltpu.VMEM((FIELDS, LAYERS, ROWS, LANES), jnp.float32),
            pltpu.VMEM((FIELDS, 6, 32, LANES), jnp.float32),
            pltpu.VMEM((32, 6, 32, LANES), jnp.float32),
            pltpu.VMEM((LANES, 2 * LANES), half),
            pltpu.VMEM((2, 3, 6, 32, LANES), half),
            pltpu.VMEM(mask.shape, jnp.int32),
            pltpu.SemaphoreType.DMA((4,)),
            pltpu.SemaphoreType.DMA((SEMAPHORES,)),
            pltpu.SemaphoreType.DMA((SEMAPHORES,)),
        ],
        compiler_params=pltpu.CompilerParams(collective_id=0, has_side_effects=True, vmem_limit_bytes=46 * 1024 * 1024),
    )(*(pltpu.with_memory_space_constraint(array, pltpu.MemorySpace.HBM) for array in (turned, mean, modes, mask)))
    return jnp.transpose(out.reshape(per, 2, 4, cz, cx, cy), (0, 1, 2, 4, 3, 5))


def solution(mesh):
    return jax.shard_map(
        shards,
        mesh=mesh,
        in_specs=(
            P("harm", None, None, "gx", "gz", None),
            P(None, "gx", "gz", None),
            P(None, None, None, "gx", "gz", None),
            P("gx", "gz", None),
        ),
        out_specs=P("harm", None, None, "gx", "gz", None),
        check_vma=False,
    )
```

```python
import jax
import jax.numpy as jnp
from jax import lax
from jax.experimental import pallas as pl
from jax.experimental.pallas import tpu as pltpu
from jax.sharding import PartitionSpec as P

FREQUENCY_STEP = 0.2
VISCOSITY = 0.05
PENALTY = 4.0
TWELFTH = 1.0 / 12.0
MESH = pl.DeviceIdType.MESH

LAYERS, ROWS, LANES = 10, 48, 128
SEMAPHORES = 56
OWN_Z = pl.ds(2, 6)
OWN_X = pl.ds(8, 32)
RIM_X = {1: pl.ds(6, 2), -1: pl.ds(40, 2)}
BARE_X = {1: pl.ds(30, 2), -1: pl.ds(0, 2)}

OWN0, LOW0, HIGH0, BASE0, FIELDS = 0, 32, 44, 56, 71


def vel(l, part, c):
    if l < 0:
        return LOW0 + ((l + 2) * 2 + part) * 3 + c
    if l > 3:
        return HIGH0 + ((l - 4) * 2 + part) * 3 + c
    return OWN0 + (l * 2 + part) * 4 + c


def base(m, part, c):
    return BASE0 + (c if m == 0 else 3 + ((m - 1) * 2 + part) * 3 + c)


MODES = [(0, 0), (1, 0), (1, 1), (2, 0), (2, 1)]
OWN = (0, 1, 2, 3)
OTHERS = (-2, -1, 4, 5)


def block(slabs, slopes, bends, mask, out, freqs, z, xb, jobs, first):
    row = xb * 8 + 8
    here = pl.ds(xb * 8, 8)

    def load(field, dz=0, dx=0):
        return slabs[field, z + 2 + dz, pl.ds(row + dx, 8), :]

    def sides(field, d):
        if d == 0:
            return tuple(load(field, 0, o) for o in (1, -1, 2, -2))
        return tuple(load(field, o, 0) for o in (1, -1, 2, -2))

    def slope(s):
        return 8.0 * (s[0] - s[1]) - (s[2] - s[3])

    def along(field, d):
        return slopes[field, z, here, :] if d == 1 else slope(sides(field, d))

    used = sorted({d for _, dirs in jobs for d in dirs})
    flow = {(m, part, d): load(base(m, part, d)) for m, part in MODES for d in used}
    solid = PENALTY * mask[z, here, :].astype(jnp.float32) if first else None
    diverge = {}
    for c in range(3):
        bend = {(m, part, d): along(base(m, part, c), d) for m, part in MODES for d in used}
        total = {}
        if not first:
            total = {(k, part): out[2 * k + part, c, z, here, :] for k in OWN for part in range(2)}

        def add(key, term):
            total[key] = total[key] + term if key in total else term

        def sub(key, term):
            total[key] = total[key] - term if key in total else -term

        for ls, dirs in jobs:
            for l in ls:
                grad = {}
                for part in range(2):
                    around = {d: sides(vel(l, part, c), d) for d in dirs if d != 1}
                    for d in dirs:
                        grad[part, d] = slopes[vel(l, part, c), z, here, :] if d == 1 else slope(around[d])
                    if l in OWN:
                        key = (l, part)
                        near = sum(side[0] + side[1] for side in around.values())
                        far = sum(side[2] + side[3] for side in around.values())
                        bent = 16.0 * near - far
                        if 1 in dirs:
                            bent = bent + bends[vel(l, part, c), z, here, :]
                        sub(key, (VISCOSITY * TWELFTH) * bent)
                        if 0 in dirs:
                            value = load(vel(l, part, c))
                            add(key, (solid + VISCOSITY * 60.0 * TWELFTH) * value)
                            turn = freqs[l] * load(vel(l, 1 - part, c))
                            (sub if part == 0 else add)(key, turn)
                        if c in dirs:
                            add(key, along(OWN0 + (l * 2 + part) * 4 + 3, c) * TWELFTH)
                            diverge[key] = diverge[key] + grad[part, c] if key in diverge else grad[part, c]
                speed = {(part, d): load(vel(l, part, d)) for part in range(2) for d in dirs}
                for k in OWN:
                    m = k - l
                    if abs(m) > 2:
                        continue
                    a = abs(m)
                    for d in dirs:
                        gr, gi = grad[0, d], grad[1, d]
                        ur, ui = speed[0, d], speed[1, d]
                        fr, br = flow[a, 0, d], bend[a, 0, d]
                        add((k, 0), fr * gr + ur * br)
                        add((k, 1), fr * gi + ui * br)
                        if a:
                            fi, bi = flow[a, 1, d], bend[a, 1, d]
                            real, imag = fi * gi + ui * bi, fi * gr + ur * bi
                            (sub if m > 0 else add)((k, 0), real)
                            (add if m > 0 else sub)((k, 1), imag)
        for key, value in total.items():
            out[2 * key[0] + key[1], c, z, here, :] = value
    for (k, part), value in diverge.items():
        value = value * TWELFTH
        out[2 * k + part, 3, z, here, :] = value if first else out[2 * k + part, 3, z, here, :] + value


def kernel(pert, mean, modes, solid_hbm, out, own, low, high, flow, slabs, slopes, bends, band, passing, solid, local_sem, send_sem, recv_sem):
    h, gx, gz = lax.axis_index("harm"), lax.axis_index("gx"), lax.axis_index("gz")
    side_x = {1: lax.rem(gx + 1, 4), -1: lax.rem(gx + 3, 4)}
    side_z = {1: lax.rem(gz + 1, 4), -1: lax.rem(gz + 3, 4)}
    odd = lax.rem(gz, 2)
    has_low, has_high = h > 0, h < 7

    barrier = pltpu.get_barrier_semaphore()

    def greet(device):
        pl.semaphore_signal(barrier, inc=1, device_id=device, device_id_type=MESH)

    for s in (1, -1):
        greet((h, side_x[s], gz))
        greet((h, gx, side_z[s]))
    greet((lax.rem(h + 4, 8), gx, 3 - gz))

    inner = jnp.logical_or(h == 3, h == 4)
    outer = jnp.logical_or(h == 0, h == 7)

    @pl.when(inner)
    def _():
        greet((7 - h, gx, 3 - gz))

    fellow = jnp.where(inner, 7 * lax.div(h, 4), 3 + lax.div(h, 4))

    @pl.when(jnp.logical_or(inner, outer))
    def _():
        greet((fellow, gx, gz))
        greet((lax.rem(h + 4, 8), gx, gz))

    @pl.when(has_low)
    def _():
        greet((h - 1, gx, gz))

    @pl.when(has_high)
    def _():
        greet((h + 1, gx, gz))

    def local(i, src, dst):
        return pltpu.make_async_copy(src, dst, local_sem.at[i])

    loads = [
        local(0, pert, own.at[:, :, OWN_Z, OWN_X]),
        local(1, mean, flow.at[pl.ds(0, 3), OWN_Z, OWN_X]),
        local(2, modes, flow.at[pl.ds(3, 12), OWN_Z, OWN_X]),
        local(3, solid_hbm, solid),
    ]
    for copy in loads:
        copy.start()

    extra = jnp.where(jnp.logical_or(inner, outer), 2, 0) + jnp.where(inner, 1, 0)
    pl.semaphore_wait(barrier, 5 + jnp.where(has_low, 1, 0) + jnp.where(has_high, 1, 0) + extra)

    counter, places = iter(range(SEMAPHORES)), {}

    def remote(src, dst, device):
        i = next(counter)
        copy = pltpu.make_async_remote_copy(
            src_ref=src, dst_ref=dst, send_sem=send_sem.at[i], recv_sem=recv_sem.at[i], device_id=device, device_id_type=MESH
        )
        places[id(copy)] = i
        return copy

    def onto(first, src, dst, device):
        return pltpu.make_async_remote_copy(
            src_ref=src,
            dst_ref=dst,
            send_sem=send_sem.at[next(counter)],
            recv_sem=recv_sem.at[places[id(first)]],
            device_id=device,
            device_id_type=MESH,
        )

    three = pl.ds(0, 3)

    up, down = [], []
    for j in range(2):
        part = pl.ds(2 * j, 2)
        up.append(remote(pert.at[pl.ds(4 + 2 * j, 2), three], low.at[part, :, OWN_Z, OWN_X], (jnp.minimum(h + 1, 7), gx, gz)))
        down.append(remote(pert.at[part, three], high.at[part, :, OWN_Z, OWN_X], (jnp.maximum(h - 1, 0), gx, gz)))
    detour, resume_up, resume_down = [], [], []
    for z in (0, 3):
        layers, inside = pl.ds(z, 3), pl.ds(2 + z, 3)
        detour.append(remote(pert.at[pl.ds(6 - 4 * lax.div(h, 4), 2), three, layers], passing.at[:, :, layers], (fellow, gx, gz)))
        resume_up.append(onto(up[1], passing.at[:, :, layers], low.at[pl.ds(2, 2), :, inside, OWN_X], (4, gx, gz)))
        resume_down.append(onto(down[1], passing.at[:, :, layers], high.at[pl.ds(2, 2), :, inside, OWN_X], (3, gx, gz)))
    rim_x, base_x, base_mate, base_off = [], [], [], []
    for s in (1, -1):
        rim_x.append(remote(pert.at[:, :, :, BARE_X[s]], own.at[:, :, OWN_Z, RIM_X[s]], (h, side_x[s], gz)))
        for ref, at, count in ((mean, 0, 3), (modes, 3, 12)):
            base_x.append(remote(ref.at[:, :, BARE_X[s]], flow.at[pl.ds(at, count), OWN_Z, RIM_X[s]], (h, side_x[s], gz)))

    off, far_off = 8 * odd, 8 * (1 - odd)
    mate = gz + 1 - 2 * odd
    to_mate, to_off = pl.ds(4 * (1 - odd), 2), pl.ds(4 * odd, 2)
    at_mate, at_off = pl.ds(8 * odd, 2), pl.ds(far_off, 2)
    rim_mate = remote(pert.at[:, :, to_mate], own.at[:, :, at_mate, OWN_X], (h, gx, mate))
    rim_off = [
        remote(pert.at[half, :, to_off], own.at[half, :, at_off, OWN_X], (h, gx, 3 - gz)) for half in (pl.ds(0, 4), pl.ds(4, 4))
    ]
    for ref, start, at, count in ((mean, 0, 0, 3), (modes, 0, 3, 6), (modes, 6, 9, 6)):
        source, fields = ref.at[pl.ds(start, count)], pl.ds(at, count)
        base_mate.append(remote(source.at[:, to_mate], flow.at[fields, at_mate, OWN_X], (h, gx, mate)))
        base_off.append(remote(source.at[:, to_off], flow.at[fields, at_off, OWN_X], (lax.rem(h + 4, 8), gx, 3 - gz)))

    def starts(copies):
        def run():
            for copy in copies:
                copy.start()

        return run

    def arrivals(copies):
        def run():
            for copy in copies:
                copy.wait_recv()

        return run

    def departures(copies):
        def run():
            for copy in copies:
                copy.wait_send()

        return run

    pl.when(inner)(starts(detour))
    pl.when(has_high)(up[0].start)
    pl.when(has_low)(down[0].start)
    cross_up, cross_down = h == 3, h == 4
    up_here, down_here = has_high & jnp.logical_not(cross_up), has_low & jnp.logical_not(cross_down)
    pl.when(up_here)(up[1].start)
    pl.when(down_here)(down[1].start)
    for copy in [*rim_x, *base_x, rim_mate, *base_mate]:
        copy.start()
    normal = jnp.logical_not(jnp.logical_or(inner, outer))
    pl.when(normal | (h == 7))(rim_off[0].start)
    pl.when(normal | (h == 0))(rim_off[1].start)
    for copy in base_off:
        copy.start()

    forward_x, forward_z, straight_z, beside_z, across_z = {}, {}, {}, {}, {}
    for name, ref, side in (("low", low, 1), ("high", high, -1)):
        harmonics = pl.ds(4, 4) if side == 1 else pl.ds(0, 4)
        target = jnp.clip(h + side, 0, 7)
        forward_x[name] = [
            remote(own.at[harmonics, three, OWN_Z, RIM_X[s]], ref.at[:, :, OWN_Z, RIM_X[s]], (target, gx, gz)) for s in (1, -1)
        ]
        rim = pl.ds(off, 2)
        forward_z[name] = remote(own.at[harmonics, three, rim, OWN_X], ref.at[:, :, rim, OWN_X], (target, gx, gz))
        straight_z[name] = onto(
            forward_z[name], pert.at[harmonics, three, to_off], ref.at[:, :, at_off, OWN_X], (target, gx, 3 - gz)
        )
        across_z[name] = onto(
            forward_z[name], ref.at[:, :, pl.ds(2 + 4 * odd, 2), OWN_X], ref.at[:, :, at_off, OWN_X], (h, gx, 3 - gz)
        )
        beside_z[name] = remote(
            ref.at[:, :, pl.ds(6 - 4 * odd, 2), OWN_X], ref.at[:, :, at_mate, OWN_X], (h, gx, mate)
        )
    pl.when(cross_up)(straight_z["low"].start)
    pl.when(cross_down)(straight_z["high"].start)
    onward_up, onward_down = has_high & jnp.logical_not(inner), has_low & jnp.logical_not(inner)

    def stage(ref, first, layers, rows, scale=None):
        groups, width = ref.shape[:2]

        def body(i, carry):
            for c in range(width):
                for z in layers:
                    for part in rows:
                        value = ref[i, c, z, part].astype(jnp.float32)
                        slabs[first + i * width + c, z, part, :] = value if scale is None else value * scale
            return carry

        lax.fori_loop(0, groups, body, 0)

    def stage_own(ref, first, curved, scale=None, span=None):
        groups, width = ref.shape[:2]
        weights = band[...] if curved else band[:, pl.ds(0, LANES)]

        def body(i, carry):
            fields = pl.ds(first + i * width, width)
            tile = ref[i, :, OWN_Z, OWN_X]
            value = tile.astype(jnp.float32)
            slabs[fields, OWN_Z, OWN_X, :] = value if scale is None else value * scale
            product = jnp.dot(tile.reshape(width * 192, LANES), weights, preferred_element_type=jnp.float32)
            if scale is not None:
                product = product * scale
            slopes[fields] = product[:, :LANES].reshape(width, 6, 32, LANES)
            if curved:
                bends[fields] = product[:, LANES:].reshape(width, 6, 32, LANES)
            return carry

        lax.fori_loop(*(span or (0, groups)), body, 0)

    middle = range(2, 8)
    flow_groups = flow.reshape(5, 3, LAYERS, ROWS, LANES)
    x_rims = (pl.ds(0, 8), pl.ds(40, 8))
    shift = lax.broadcasted_iota(jnp.int32, (LANES, LANES), 0) - lax.broadcasted_iota(jnp.int32, (LANES, LANES), 1)
    first_band, second_band = jnp.zeros((LANES, LANES), jnp.float32), jnp.zeros((LANES, LANES), jnp.float32)
    for offset, one, two in ((1, 8.0, 16.0), (-1, -8.0, 16.0), (2, -1.0, -1.0), (-2, 1.0, -1.0), (0, 0.0, -30.0)):
        first_band = jnp.where(shift == offset, one, first_band)
        second_band = jnp.where(shift == offset, two, second_band)
    band[:, pl.ds(0, LANES)] = first_band.astype(band.dtype)
    band[:, pl.ds(LANES, LANES)] = second_band.astype(band.dtype)
    for copy in loads:
        copy.wait()
    stage_own(own, OWN0, True)
    stage_own(flow_groups, BASE0, False, TWELFTH)

    freqs = [FREQUENCY_STEP * (h * 4 + k - 16).astype(jnp.float32) for k in range(4)]

    def sweep(jobs, first=False, layers=(0, 6), chunks=(0, 1, 4), finish=None):
        start, step, count = chunks

        def layer(j, carry):
            z = layers[0] + j

            def chunk(i, inner_carry):
                block(slabs, slopes, bends, solid, out, freqs, z, start + step * i, jobs, first)
                return inner_carry

            lax.fori_loop(0, count, chunk, 0)
            if finish is not None:
                finish(j)
            return carry

        lax.fori_loop(0, layers[1], layer, 0)

    free, bound = (2 - 2 * odd, 4), (4 * odd, 2)
    mate_edge, off_edge = [far_off, far_off + 1], [off, off + 1]

    def pass_half(i):
        detour[i].wait_recv()
        pl.when(h == 0)(resume_up[i].start)
        pl.when(h == 7)(resume_down[i].start)

    sweep([(OWN, (0, 1))], True, chunks=(1, 1, 2))

    @pl.when(outer)
    def _():
        pass_half(0)

    arrivals(rim_x)()
    pl.when(has_high)(starts(forward_x["low"]))
    pl.when(has_low)(starts(forward_x["high"]))
    pl.when(inner)(starts(rim_off))
    arrivals(base_x)()
    stage(own, OWN0, middle, x_rims)
    stage(flow_groups, BASE0, middle, x_rims, TWELFTH)

    def pass_on(j):
        @pl.when(outer & (j == 2))
        def _():
            pass_half(1)
            pl.when(h == 0)(rim_off[0].start)
            pl.when(h == 7)(rim_off[1].start)

    sweep([(OWN, (0, 1))], True, chunks=(0, 3, 2), finish=pass_on)
    arrivals([rim_mate, *base_mate])()
    stage(own, OWN0, mate_edge, (OWN_X,))
    stage(flow_groups, BASE0, mate_edge, (OWN_X,), TWELFTH)
    sweep([(OWN, (2,))], layers=free)

    @pl.when(jnp.logical_not(inner))
    def _():
        pl.when(h != 0)(rim_off[0].wait_recv)
        pl.when(h != 7)(rim_off[1].wait_recv)
        pl.when(onward_up)(forward_z["low"].start)
        pl.when(onward_down)(forward_z["high"].start)

    def own_bound():
        arrivals(base_off)()
        stage(own, OWN0, off_edge, (OWN_X,))
        stage(flow_groups, BASE0, off_edge, (OWN_X,), TWELFTH)
        sweep([(OWN, (2,))], layers=bound)

    pl.when(normal)(own_bound)
    both = ((has_low, up, low, "low", LOW0, h == 5), (has_high, down, high, "high", HIGH0, h == 2))
    for j in range(2):
        for present, copies, ref, name, first, there in both:

            @pl.when(present)
            def _(copies=copies, ref=ref, name=name, first=first):
                copies[j].wait_recv()
                if j == 1:
                    beside_z[name].start()

            if j == 1:
                pl.when(there)(across_z[name].start)

            @pl.when(present)
            def _(ref=ref, first=first):
                stage_own(ref, first, False, span=(2 * j, 2 * j + 2))

    for present, _, ref, name, first, _ in both:

        @pl.when(present)
        def _(ref=ref, name=name, first=first):
            arrivals(forward_x[name])()
            stage(ref, first, middle, x_rims)

        @pl.when(jnp.logical_not(present))
        def _(first=first):
            def clear(i, carry):
                slabs[first + i] = jnp.zeros((LAYERS, ROWS, LANES), jnp.float32)
                slopes[first + i] = jnp.zeros((6, 32, LANES), jnp.float32)
                return carry

            lax.fori_loop(0, 12, clear, 0)

    sweep([(OTHERS, (0, 1))], layers=bound)
    for present, _, ref, name, first, _ in both:

        @pl.when(present)
        def _(ref=ref, name=name, first=first):
            beside_z[name].wait_recv()
            stage(ref, first, mate_edge, (OWN_X,))

    sweep([(OTHERS, (0, 1, 2))], layers=free)
    pl.when(inner | (h == 0))(rim_off[0].wait_recv)
    pl.when(inner | (h == 7))(rim_off[1].wait_recv)
    pl.when(jnp.logical_not(normal))(own_bound)
    for present, ref, name, first in ((has_low, low, "low", LOW0), (has_high, high, "high", HIGH0)):

        @pl.when(present)
        def _(ref=ref, name=name, first=first):
            forward_z[name].wait_recv()
            stage(ref, first, off_edge, (OWN_X,))

    sweep([(OTHERS, (2,))], layers=bound)
    departures([*rim_x, *base_x, rim_mate, *rim_off, *base_mate, *base_off])()
    pl.when(inner)(departures(detour))
    pl.when(h == 0)(departures(resume_up))
    pl.when(h == 7)(departures(resume_down))
    pl.when(has_high)(up[0].wait_send)
    pl.when(has_low)(down[0].wait_send)
    pl.when(up_here)(up[1].wait_send)
    pl.when(down_here)(down[1].wait_send)
    for goes, onward, name in ((has_high, onward_up, "low"), (has_low, onward_down, "high")):
        pl.when(goes)(departures(forward_x[name]))
        pl.when(onward)(forward_z[name].wait_send)
    pl.when(cross_up)(straight_z["low"].wait_send)
    pl.when(cross_down)(straight_z["high"].wait_send)
    pl.when(h == 5)(across_z["low"].wait_send)
    pl.when(h == 2)(across_z["high"].wait_send)
    for present, name in ((has_low, "low"), (has_high, "high")):
        pl.when(present)(beside_z[name].wait_send)


def shards(perturbation, base_mean, base_modes, solid_mask):
    per, _, _, cx, cz, cy = perturbation.shape
    turned = jnp.transpose(perturbation, (0, 1, 2, 4, 3, 5)).reshape(per * 2, 4, cz, cx, cy)
    mean = jnp.transpose(base_mean, (0, 2, 1, 3))
    modes = jnp.transpose(base_modes, (0, 1, 2, 4, 3, 5)).reshape(12, cz, cx, cy)
    mask = jnp.transpose(solid_mask, (1, 0, 2))
    anywhere = pl.BlockSpec(memory_space=pl.ANY)
    vmem = pl.BlockSpec(memory_space=pltpu.VMEM)
    half = jnp.bfloat16
    out = pl.pallas_call(
        kernel,
        out_shape=jax.ShapeDtypeStruct(turned.shape, jnp.float32),
        in_specs=[anywhere] * 4,
        out_specs=vmem,
        scratch_shapes=[
            pltpu.VMEM((8, 4, LAYERS, ROWS, LANES), half),
            pltpu.VMEM((4, 3, LAYERS, ROWS, LANES), half),
            pltpu.VMEM((4, 3, LAYERS, ROWS, LANES), half),
            pltpu.VMEM((15, LAYERS, ROWS, LANES), half),
            pltpu.VMEM((FIELDS, LAYERS, ROWS, LANES), jnp.float32),
            pltpu.VMEM((FIELDS, 6, 32, LANES), jnp.float32),
            pltpu.VMEM((32, 6, 32, LANES), jnp.float32),
            pltpu.VMEM((LANES, 2 * LANES), half),
            pltpu.VMEM((2, 3, 6, 32, LANES), half),
            pltpu.VMEM(mask.shape, jnp.int32),
            pltpu.SemaphoreType.DMA((4,)),
            pltpu.SemaphoreType.DMA((SEMAPHORES,)),
            pltpu.SemaphoreType.DMA((SEMAPHORES,)),
        ],
        compiler_params=pltpu.CompilerParams(collective_id=0, has_side_effects=True, vmem_limit_bytes=46 * 1024 * 1024),
    )(*(pltpu.with_memory_space_constraint(array, pltpu.MemorySpace.HBM) for array in (turned, mean, modes, mask)))
    return jnp.transpose(out.reshape(per, 2, 4, cz, cx, cy), (0, 1, 2, 4, 3, 5))


def solution(mesh):
    return jax.shard_map(
        shards,
        mesh=mesh,
        in_specs=(
            P("harm", None, None, "gx", "gz", None),
            P(None, "gx", "gz", None),
            P(None, None, None, "gx", "gz", None),
            P("gx", "gz", None),
        ),
        out_specs=P("harm", None, None, "gx", "gz", None),
        check_vma=False,
    )
```

```python
import jax
import jax.numpy as jnp
from jax import lax
from jax.experimental import pallas as pl
from jax.experimental.pallas import tpu as pltpu
from jax.sharding import PartitionSpec as P

FREQUENCY_STEP = 0.2
VISCOSITY = 0.05
PENALTY = 4.0
TWELFTH = 1.0 / 12.0
MESH = pl.DeviceIdType.MESH

LAYERS, ROWS, LANES = 10, 48, 128
SEMAPHORES = 56
OWN_Z = pl.ds(2, 6)
OWN_X = pl.ds(8, 32)
RIM_X = {1: pl.ds(6, 2), -1: pl.ds(40, 2)}
BARE_X = {1: pl.ds(30, 2), -1: pl.ds(0, 2)}

OWN0, LOW0, HIGH0, BASE0, FIELDS = 0, 32, 44, 56, 71


def vel(l, part, c):
    if l < 0:
        return LOW0 + ((l + 2) * 2 + part) * 3 + c
    if l > 3:
        return HIGH0 + ((l - 4) * 2 + part) * 3 + c
    return OWN0 + (l * 2 + part) * 4 + c


def base(m, part, c):
    return BASE0 + (c if m == 0 else 3 + ((m - 1) * 2 + part) * 3 + c)


MODES = [(0, 0), (1, 0), (1, 1), (2, 0), (2, 1)]
OWN = (0, 1, 2, 3)
OTHERS = (-2, -1, 4, 5)


def block(slabs, slopes, bends, mask, out, freqs, z, xb, jobs, first):
    row = xb * 8 + 8
    here = pl.ds(xb * 8, 8)

    def load(field, dz=0, dx=0):
        return slabs[field, z + 2 + dz, pl.ds(row + dx, 8), :]

    def sides(field, d):
        if d == 0:
            return tuple(load(field, 0, o) for o in (1, -1, 2, -2))
        return tuple(load(field, o, 0) for o in (1, -1, 2, -2))

    def slope(s):
        return 8.0 * (s[0] - s[1]) - (s[2] - s[3])

    def along(field, d):
        return slopes[field, z, here, :] if d == 1 else slope(sides(field, d))

    used = sorted({d for _, dirs in jobs for d in dirs})
    flow = {(m, part, d): load(base(m, part, d)) for m, part in MODES for d in used}
    solid = PENALTY * mask[z, here, :].astype(jnp.float32) if first else None
    diverge = {}
    for c in range(3):
        bend = {(m, part, d): along(base(m, part, c), d) for m, part in MODES for d in used}
        total = {}
        if not first:
            total = {(k, part): out[2 * k + part, c, z, here, :] for k in OWN for part in range(2)}

        def add(key, term):
            total[key] = total[key] + term if key in total else term

        def sub(key, term):
            total[key] = total[key] - term if key in total else -term

        for ls, dirs in jobs:
            for l in ls:
                grad = {}
                for part in range(2):
                    around = {d: sides(vel(l, part, c), d) for d in dirs if d != 1}
                    for d in dirs:
                        grad[part, d] = slopes[vel(l, part, c), z, here, :] if d == 1 else slope(around[d])
                    if l in OWN:
                        key = (l, part)
                        near = sum(side[0] + side[1] for side in around.values())
                        far = sum(side[2] + side[3] for side in around.values())
                        bent = 16.0 * near - far
                        if 1 in dirs:
                            bent = bent + bends[vel(l, part, c), z, here, :]
                        sub(key, (VISCOSITY * TWELFTH) * bent)
                        if 0 in dirs:
                            value = load(vel(l, part, c))
                            add(key, (solid + VISCOSITY * 60.0 * TWELFTH) * value)
                            turn = freqs[l] * load(vel(l, 1 - part, c))
                            (sub if part == 0 else add)(key, turn)
                        if c in dirs:
                            add(key, along(OWN0 + (l * 2 + part) * 4 + 3, c) * TWELFTH)
                            diverge[key] = diverge[key] + grad[part, c] if key in diverge else grad[part, c]
                speed = {(part, d): load(vel(l, part, d)) for part in range(2) for d in dirs}
                for k in OWN:
                    m = k - l
                    if abs(m) > 2:
                        continue
                    a = abs(m)
                    for d in dirs:
                        gr, gi = grad[0, d], grad[1, d]
                        ur, ui = speed[0, d], speed[1, d]
                        fr, br = flow[a, 0, d], bend[a, 0, d]
                        add((k, 0), fr * gr + ur * br)
                        add((k, 1), fr * gi + ui * br)
                        if a:
                            fi, bi = flow[a, 1, d], bend[a, 1, d]
                            real, imag = fi * gi + ui * bi, fi * gr + ur * bi
                            (sub if m > 0 else add)((k, 0), real)
                            (add if m > 0 else sub)((k, 1), imag)
        for key, value in total.items():
            out[2 * key[0] + key[1], c, z, here, :] = value
    for (k, part), value in diverge.items():
        value = value * TWELFTH
        out[2 * k + part, 3, z, here, :] = value if first else out[2 * k + part, 3, z, here, :] + value


def kernel(pert, mean, modes, solid_hbm, out, own, low, high, flow, slabs, slopes, bends, band, passing, solid, local_sem, send_sem, recv_sem):
    h, gx, gz = lax.axis_index("harm"), lax.axis_index("gx"), lax.axis_index("gz")
    side_x = {1: lax.rem(gx + 1, 4), -1: lax.rem(gx + 3, 4)}
    side_z = {1: lax.rem(gz + 1, 4), -1: lax.rem(gz + 3, 4)}
    odd = lax.rem(gz, 2)
    has_low, has_high = h > 0, h < 7

    barrier = pltpu.get_barrier_semaphore()

    def greet(device):
        pl.semaphore_signal(barrier, inc=1, device_id=device, device_id_type=MESH)

    for s in (1, -1):
        greet((h, side_x[s], gz))
        greet((h, gx, side_z[s]))
    greet((lax.rem(h + 4, 8), gx, 3 - gz))

    inner = jnp.logical_or(h == 3, h == 4)
    outer = jnp.logical_or(h == 0, h == 7)

    @pl.when(inner)
    def _():
        greet((7 - h, gx, 3 - gz))

    fellow = jnp.where(inner, 7 * lax.div(h, 4), 3 + lax.div(h, 4))

    @pl.when(jnp.logical_or(inner, outer))
    def _():
        greet((fellow, gx, gz))
        greet((lax.rem(h + 4, 8), gx, gz))

    @pl.when(has_low)
    def _():
        greet((h - 1, gx, gz))

    @pl.when(has_high)
    def _():
        greet((h + 1, gx, gz))

    def local(i, src, dst):
        return pltpu.make_async_copy(src, dst, local_sem.at[i])

    loads = [
        local(0, pert, own.at[:, :, OWN_Z, OWN_X]),
        local(1, mean, flow.at[pl.ds(0, 3), OWN_Z, OWN_X]),
        local(2, modes, flow.at[pl.ds(3, 12), OWN_Z, OWN_X]),
        local(3, solid_hbm, solid),
    ]
    for copy in loads:
        copy.start()

    extra = jnp.where(jnp.logical_or(inner, outer), 2, 0) + jnp.where(inner, 1, 0)
    pl.semaphore_wait(barrier, 5 + jnp.where(has_low, 1, 0) + jnp.where(has_high, 1, 0) + extra)

    counter, places = iter(range(SEMAPHORES)), {}

    def remote(src, dst, device):
        i = next(counter)
        copy = pltpu.make_async_remote_copy(
            src_ref=src, dst_ref=dst, send_sem=send_sem.at[i], recv_sem=recv_sem.at[i], device_id=device, device_id_type=MESH
        )
        places[id(copy)] = i
        return copy

    def onto(first, src, dst, device):
        return pltpu.make_async_remote_copy(
            src_ref=src,
            dst_ref=dst,
            send_sem=send_sem.at[next(counter)],
            recv_sem=recv_sem.at[places[id(first)]],
            device_id=device,
            device_id_type=MESH,
        )

    three = pl.ds(0, 3)

    up, down = [], []
    for j in range(2):
        part = pl.ds(2 * j, 2)
        up.append(remote(pert.at[pl.ds(4 + 2 * j, 2), three], low.at[part, :, OWN_Z, OWN_X], (jnp.minimum(h + 1, 7), gx, gz)))
        down.append(remote(pert.at[part, three], high.at[part, :, OWN_Z, OWN_X], (jnp.maximum(h - 1, 0), gx, gz)))
    detour, resume_up, resume_down = [], [], []
    for z in (0, 3):
        layers, inside = pl.ds(z, 3), pl.ds(2 + z, 3)
        detour.append(remote(pert.at[pl.ds(6 - 4 * lax.div(h, 4), 2), three, layers], passing.at[:, :, layers], (fellow, gx, gz)))
        resume_up.append(onto(up[1], passing.at[:, :, layers], low.at[pl.ds(2, 2), :, inside, OWN_X], (4, gx, gz)))
        resume_down.append(onto(down[1], passing.at[:, :, layers], high.at[pl.ds(2, 2), :, inside, OWN_X], (3, gx, gz)))
    rim_x, base_x, base_mate, base_off = [], [], [], []
    for s in (1, -1):
        rim_x.append(remote(pert.at[:, :, :, BARE_X[s]], own.at[:, :, OWN_Z, RIM_X[s]], (h, side_x[s], gz)))
        for ref, at, count in ((mean, 0, 3), (modes, 3, 12)):
            base_x.append(remote(ref.at[:, :, BARE_X[s]], flow.at[pl.ds(at, count), OWN_Z, RIM_X[s]], (h, side_x[s], gz)))

    off, far_off = 8 * odd, 8 * (1 - odd)
    mate = gz + 1 - 2 * odd
    to_mate, to_off = pl.ds(4 * (1 - odd), 2), pl.ds(4 * odd, 2)
    at_mate, at_off = pl.ds(8 * odd, 2), pl.ds(far_off, 2)
    rim_mate = remote(pert.at[:, :, to_mate], own.at[:, :, at_mate, OWN_X], (h, gx, mate))
    rim_off = [
        remote(pert.at[half, :, to_off], own.at[half, :, at_off, OWN_X], (h, gx, 3 - gz)) for half in (pl.ds(0, 4), pl.ds(4, 4))
    ]
    for ref, start, at, count in ((mean, 0, 0, 3), (modes, 0, 3, 6), (modes, 6, 9, 6)):
        source, fields = ref.at[pl.ds(start, count)], pl.ds(at, count)
        base_mate.append(remote(source.at[:, to_mate], flow.at[fields, at_mate, OWN_X], (h, gx, mate)))
        base_off.append(remote(source.at[:, to_off], flow.at[fields, at_off, OWN_X], (lax.rem(h + 4, 8), gx, 3 - gz)))

    def starts(copies):
        def run():
            for copy in copies:
                copy.start()

        return run

    def arrivals(copies):
        def run():
            for copy in copies:
                copy.wait_recv()

        return run

    def departures(copies):
        def run():
            for copy in copies:
                copy.wait_send()

        return run

    pl.when(inner)(starts(detour))
    pl.when(has_high)(up[0].start)
    pl.when(has_low)(down[0].start)
    cross_up, cross_down = h == 3, h == 4
    up_here, down_here = has_high & jnp.logical_not(cross_up), has_low & jnp.logical_not(cross_down)
    pl.when(up_here)(up[1].start)
    pl.when(down_here)(down[1].start)
    for copy in [*rim_x, *base_x, rim_mate, *base_mate]:
        copy.start()
    normal = jnp.logical_not(jnp.logical_or(inner, outer))
    pl.when(normal | (h == 7))(rim_off[0].start)
    pl.when(normal | (h == 0))(rim_off[1].start)
    for copy in base_off:
        copy.start()

    forward_x, forward_z, straight_z, beside_z, across_z = {}, {}, {}, {}, {}
    for name, ref, side in (("low", low, 1), ("high", high, -1)):
        harmonics = pl.ds(4, 4) if side == 1 else pl.ds(0, 4)
        target = jnp.clip(h + side, 0, 7)
        forward_x[name] = [
            remote(own.at[harmonics, three, OWN_Z, RIM_X[s]], ref.at[:, :, OWN_Z, RIM_X[s]], (target, gx, gz)) for s in (1, -1)
        ]
        rim = pl.ds(off, 2)
        forward_z[name] = remote(own.at[harmonics, three, rim, OWN_X], ref.at[:, :, rim, OWN_X], (target, gx, gz))
        straight_z[name] = onto(
            forward_z[name], pert.at[harmonics, three, to_off], ref.at[:, :, at_off, OWN_X], (target, gx, 3 - gz)
        )
        across_z[name] = onto(
            forward_z[name], ref.at[:, :, pl.ds(2 + 4 * odd, 2), OWN_X], ref.at[:, :, at_off, OWN_X], (h, gx, 3 - gz)
        )
        beside_z[name] = remote(
            ref.at[:, :, pl.ds(6 - 4 * odd, 2), OWN_X], ref.at[:, :, at_mate, OWN_X], (h, gx, mate)
        )
    pl.when(cross_up)(straight_z["low"].start)
    pl.when(cross_down)(straight_z["high"].start)
    onward_up, onward_down = has_high & jnp.logical_not(inner), has_low & jnp.logical_not(inner)

    def stage(ref, first, layers, rows, scale=None, span=None):
        groups, width = ref.shape[:2]

        def body(i, carry):
            for c in range(width):
                for z in layers:
                    for part in rows:
                        value = ref[i, c, z, part].astype(jnp.float32)
                        slabs[first + i * width + c, z, part, :] = value if scale is None else value * scale
            return carry

        lax.fori_loop(*(span or (0, groups)), body, 0)

    def stage_own(ref, first, curved, scale=None, span=None):
        groups, width = ref.shape[:2]
        weights = band[...] if curved else band[:, pl.ds(0, LANES)]

        def body(i, carry):
            fields = pl.ds(first + i * width, width)
            tile = ref[i, :, OWN_Z, OWN_X]
            value = tile.astype(jnp.float32)
            slabs[fields, OWN_Z, OWN_X, :] = value if scale is None else value * scale
            product = jnp.dot(tile.reshape(width * 192, LANES), weights, preferred_element_type=jnp.float32)
            if scale is not None:
                product = product * scale
            slopes[fields] = product[:, :LANES].reshape(width, 6, 32, LANES)
            if curved:
                bends[fields] = product[:, LANES:].reshape(width, 6, 32, LANES)
            return carry

        lax.fori_loop(*(span or (0, groups)), body, 0)

    middle = range(2, 8)
    flow_groups = flow.reshape(5, 3, LAYERS, ROWS, LANES)
    x_rims = (pl.ds(0, 8), pl.ds(40, 8))
    shift = lax.broadcasted_iota(jnp.int32, (LANES, LANES), 0) - lax.broadcasted_iota(jnp.int32, (LANES, LANES), 1)
    first_band, second_band = jnp.zeros((LANES, LANES), jnp.float32), jnp.zeros((LANES, LANES), jnp.float32)
    for offset, one, two in ((1, 8.0, 16.0), (-1, -8.0, 16.0), (2, -1.0, -1.0), (-2, 1.0, -1.0), (0, 0.0, -30.0)):
        first_band = jnp.where(shift == offset, one, first_band)
        second_band = jnp.where(shift == offset, two, second_band)
    band[:, pl.ds(0, LANES)] = first_band.astype(band.dtype)
    band[:, pl.ds(LANES, LANES)] = second_band.astype(band.dtype)
    for copy in loads:
        copy.wait()
    stage_own(own, OWN0, True)
    stage_own(flow_groups, BASE0, False, TWELFTH)

    freqs = [FREQUENCY_STEP * (h * 4 + k - 16).astype(jnp.float32) for k in range(4)]

    def sweep(jobs, first=False, layers=(0, 6), chunks=(0, 1, 4), finish=None):
        start, step, count = chunks

        def layer(j, carry):
            z = layers[0] + j

            def chunk(i, inner_carry):
                block(slabs, slopes, bends, solid, out, freqs, z, start + step * i, jobs, first)
                return inner_carry

            lax.fori_loop(0, count, chunk, 0)
            if finish is not None:
                finish(j)
            return carry

        lax.fori_loop(0, layers[1], layer, 0)

    free, bound = (2 - 2 * odd, 4), (4 * odd, 2)
    mate_edge, off_edge = [far_off, far_off + 1], [off, off + 1]

    def pass_half(i):
        detour[i].wait_recv()
        pl.when(h == 0)(resume_up[i].start)
        pl.when(h == 7)(resume_down[i].start)

    def pass_first(j):
        @pl.when(outer & (j == 4))
        def _():
            pass_half(0)

    sweep([(OWN, (0, 1))], True, chunks=(1, 1, 2), finish=pass_first)
    arrivals(rim_x)()
    pl.when(has_high)(starts(forward_x["low"]))
    pl.when(has_low)(starts(forward_x["high"]))
    pl.when(inner)(starts(rim_off))
    arrivals(base_x)()
    stage(own, OWN0, middle, x_rims)
    stage(flow_groups, BASE0, middle, x_rims, TWELFTH)

    def pass_on(j):
        @pl.when(outer & (j == 1))
        def _():
            pass_half(1)
            pl.when(h == 0)(rim_off[0].start)
            pl.when(h == 7)(rim_off[1].start)

    sweep([(OWN, (0, 1))], True, chunks=(0, 3, 2), finish=pass_on)
    arrivals([rim_mate, *base_mate])()
    stage(own, OWN0, mate_edge, (OWN_X,))
    stage(flow_groups, BASE0, mate_edge, (OWN_X,), TWELFTH)
    sweep([(OWN, (2,))], layers=free)

    @pl.when(jnp.logical_not(inner))
    def _():
        pl.when(h != 0)(rim_off[0].wait_recv)
        pl.when(h != 7)(rim_off[1].wait_recv)
        pl.when(onward_up)(forward_z["low"].start)
        pl.when(onward_down)(forward_z["high"].start)

    def own_bound():
        arrivals(base_off)()
        stage(own, OWN0, off_edge, (OWN_X,))
        stage(flow_groups, BASE0, off_edge, (OWN_X,), TWELFTH)
        sweep([(OWN, (2,))], layers=bound)

    pl.when(normal)(own_bound)
    both = ((has_low, up, low, "low", LOW0, h == 5), (has_high, down, high, "high", HIGH0, h == 2))
    for j in range(2):
        for present, copies, ref, name, first, there in both:

            @pl.when(present)
            def _(copies=copies, ref=ref, name=name, first=first):
                copies[j].wait_recv()
                if j == 1:
                    beside_z[name].start()

            if j == 1:
                pl.when(there)(across_z[name].start)

            @pl.when(present)
            def _(ref=ref, first=first):
                stage_own(ref, first, False, span=(2 * j, 2 * j + 2))

    for present, _, ref, name, first, _ in both:

        @pl.when(present)
        def _(ref=ref, name=name, first=first):
            arrivals(forward_x[name])()
            stage(ref, first, middle, x_rims)

    cases = (
        (normal | inner, [(OTHERS, (0, 1))], [(OTHERS, (0, 1, 2))], [(OTHERS, (2,))]),
        (h == 0, [((4, 5), (0, 1))], [((4, 5), (0, 1, 2))], [((4, 5), (2,))]),
        (h == 7, [((-2, -1), (0, 1))], [((-2, -1), (0, 1, 2))], [((-2, -1), (2,))]),
    )
    for case, plane, _, _ in cases:
        pl.when(case)(lambda plane=plane: sweep(plane, layers=bound))
    for present, _, ref, name, first, _ in both:

        @pl.when(present)
        def _(ref=ref, name=name, first=first):
            beside_z[name].wait_recv()
            stage(ref, first, mate_edge, (OWN_X,))

    for case, _, inside, _ in cases:
        pl.when(case)(lambda inside=inside: sweep(inside, layers=free))
    pl.when(inner | (h == 0))(rim_off[0].wait_recv)
    pl.when(inner | (h == 7))(rim_off[1].wait_recv)
    pl.when(jnp.logical_not(normal))(own_bound)
    for present, ref, name, first in ((has_low, low, "low", LOW0), (has_high, high, "high", HIGH0)):

        @pl.when(present)
        def _(ref=ref, name=name, first=first):
            forward_z[name].wait_recv()
            stage(ref, first, off_edge, (OWN_X,))

    for case, _, _, last in cases:
        pl.when(case)(lambda last=last: sweep(last, layers=bound))
    departures([*rim_x, *base_x, rim_mate, *rim_off, *base_mate, *base_off])()
    pl.when(inner)(departures(detour))
    pl.when(h == 0)(departures(resume_up))
    pl.when(h == 7)(departures(resume_down))
    pl.when(has_high)(up[0].wait_send)
    pl.when(has_low)(down[0].wait_send)
    pl.when(up_here)(up[1].wait_send)
    pl.when(down_here)(down[1].wait_send)
    for goes, onward, name in ((has_high, onward_up, "low"), (has_low, onward_down, "high")):
        pl.when(goes)(departures(forward_x[name]))
        pl.when(onward)(forward_z[name].wait_send)
    pl.when(cross_up)(straight_z["low"].wait_send)
    pl.when(cross_down)(straight_z["high"].wait_send)
    pl.when(h == 5)(across_z["low"].wait_send)
    pl.when(h == 2)(across_z["high"].wait_send)
    for present, name in ((has_low, "low"), (has_high, "high")):
        pl.when(present)(beside_z[name].wait_send)


def shards(perturbation, base_mean, base_modes, solid_mask):
    per, _, _, cx, cz, cy = perturbation.shape
    turned = jnp.transpose(perturbation, (0, 1, 2, 4, 3, 5)).reshape(per * 2, 4, cz, cx, cy)
    mean = jnp.transpose(base_mean, (0, 2, 1, 3))
    modes = jnp.transpose(base_modes, (0, 1, 2, 4, 3, 5)).reshape(12, cz, cx, cy)
    mask = jnp.transpose(solid_mask, (1, 0, 2))
    anywhere = pl.BlockSpec(memory_space=pl.ANY)
    vmem = pl.BlockSpec(memory_space=pltpu.VMEM)
    half = jnp.bfloat16
    out = pl.pallas_call(
        kernel,
        out_shape=jax.ShapeDtypeStruct(turned.shape, jnp.float32),
        in_specs=[anywhere] * 4,
        out_specs=vmem,
        scratch_shapes=[
            pltpu.VMEM((8, 4, LAYERS, ROWS, LANES), half),
            pltpu.VMEM((4, 3, LAYERS, ROWS, LANES), half),
            pltpu.VMEM((4, 3, LAYERS, ROWS, LANES), half),
            pltpu.VMEM((15, LAYERS, ROWS, LANES), half),
            pltpu.VMEM((FIELDS, LAYERS, ROWS, LANES), jnp.float32),
            pltpu.VMEM((FIELDS, 6, 32, LANES), jnp.float32),
            pltpu.VMEM((32, 6, 32, LANES), jnp.float32),
            pltpu.VMEM((LANES, 2 * LANES), half),
            pltpu.VMEM((2, 3, 6, 32, LANES), half),
            pltpu.VMEM(mask.shape, jnp.int32),
            pltpu.SemaphoreType.DMA((4,)),
            pltpu.SemaphoreType.DMA((SEMAPHORES,)),
            pltpu.SemaphoreType.DMA((SEMAPHORES,)),
        ],
        compiler_params=pltpu.CompilerParams(
            collective_id=0,
            has_side_effects=True,
            vmem_limit_bytes=46 * 1024 * 1024,
        ),
    )(*(pltpu.with_memory_space_constraint(array, pltpu.MemorySpace.HBM) for array in (turned, mean, modes, mask)))
    return jnp.transpose(out.reshape(per, 2, 4, cz, cx, cy), (0, 1, 2, 4, 3, 5))


def solution(mesh):
    return jax.shard_map(
        shards,
        mesh=mesh,
        in_specs=(
            P("harm", None, None, "gx", "gz", None),
            P(None, "gx", "gz", None),
            P(None, None, None, "gx", "gz", None),
            P("gx", "gz", None),
        ),
        out_specs=P("harm", None, None, "gx", "gz", None),
        check_vma=False,
    )
```
